512 devices in a mesh: site: 16 (over z, core), col: 32 (over x, y).
Axes of the slice: x: 4, y: 8, z: 8, core: 2. Of those that a mesh axis runs over, the one named last changes fastest.
Arguments:
- state_prev: float32 [128, 128, 8192], P('site', None, 'col'), may hold values from -6 to 6
- state_cur: float32 [128, 128, 8192], P('site', None, 'col'), may hold values from -6 to 6
- occupancy: int32 [4, 128, 128], replicated, may hold values 0 or 1
- panel_order: int32 [32], replicated, may hold values from 0 to 31, each once
Outputs:
- ortho_states: float32 [128, 128, 8192], P('site', None, 'col')
- growth: float32 [2, 256], replicated
The draws below stay inside these ranges and needn't reach their ends.
Inputs may be any that keep to these rules, and one draw needn't show every extreme that they name: panel_order holds each panel number once.
All inputs are finite; a program needn't handle non-finite values.
Results may differ from the reference program's by a relative error of at most 0.000075.
Values sent between devices are 32-bit elements; how exact they have to be, the bound alone decides.
No kernel may reach another device: no remote copies, remote signals or barrier semaphores. Data moves between devices by JAX's collectives and lax.ppermute only.
A program may use at most 64 MiB of HBM per device.

```python
import jax
import jax.numpy as jnp
from jax import lax

L = 128
STEPS = 4
PANEL = 256
COLS = 8192
PANELS = 32


def touch_ends(values, key, low, high):
    dims = values.shape
    place = [jax.random.randint(jax.random.fold_in(key, axis), (), 0, dims[axis]) for axis in range(len(dims))]
    values = values.at[tuple(place)].set(low)
    longest = dims.index(max(dims))
    place[longest] = (place[longest] + 1) % dims[longest]
    return values.at[tuple(place)].set(high)


def block_scale(stream_key, dims, pieces, smallest, top_value):
    gain = 1.0
    for position, shards_of in pieces:
        heights = jax.random.uniform(jax.random.fold_in(jax.random.fold_in(stream_key, 6), position), (shards_of,), jnp.float32, smallest / len(pieces), top_value / len(pieces))
        gain = gain * jnp.repeat(jnp.exp(heights), dims[position] // shards_of).reshape((-1,) + (1,) * (len(dims) - 1 - position))
    return gain


def centred(rng, extent, scale, most, pieces=(), dtype=jnp.bfloat16):
    values = jax.random.normal(rng, extent, jnp.float32) * scale
    if len(pieces) > 0:
        values = block_scale(rng, extent, pieces, -0.22, 0.18) * values
    return jnp.clip(values, min=-most, max=most).astype(dtype)


def setup_inputs(seed: int = 0) -> dict:
    key_of = jax.random.split(jax.random.key(seed), 5)
    state_prev = centred(key_of[0], (L, L, COLS), 1.0, 6.0, ((0, 16), (2, 32)), jnp.float32)
    state_cur = centred(key_of[1], (L, L, COLS), 1.0, 6.0, ((0, 16), (2, 32)), jnp.float32)
    occupancy = touch_ends((jax.random.randint(key_of[2], (STEPS, L, L), 0, 10) < 7).astype(jnp.int32), jax.random.fold_in(key_of[2], 1), 0, 1)
    panel_order = jax.random.permutation(key_of[3], PANELS).astype(jnp.int32)
    return dict(state_prev=state_prev, state_cur=state_cur, occupancy=occupancy, panel_order=panel_order)


ENERGY = 0.5
RESCALE = 0.015625

def product(left, right):
    return jnp.dot(left.astype(jnp.float32), right.astype(jnp.float32), precision=lax.Precision.HIGHEST, preferred_element_type=jnp.float32)

def advance(previous, current, present):
    weights = present.astype(jnp.float32)[:, :, None]
    neighbours = jnp.roll(current, 1, 0) + jnp.roll(current, -1, 0) + jnp.roll(current, 1, 1) + jnp.roll(current, -1, 1)
    return (current, weights * (ENERGY * current - neighbours - previous))

def orthogonalize(block):
    lower = jnp.linalg.cholesky(product(block.T, block))
    return (lower, jax.scipy.linalg.solve_triangular(lower, block.T, lower=True).T)

def reference(state_prev, state_cur, occupancy, panel_order):
    previous, current = (state_prev, state_cur)
    for turn in range(STEPS):
        previous, current = advance(previous, current, occupancy[turn])
    flat = current.reshape(L * L, COLS)
    first_start = (panel_order[0] * PANEL).astype(jnp.int32)
    second_start = (panel_order[1] * PANEL).astype(jnp.int32)
    first_lower, first_q = orthogonalize(lax.dynamic_slice_in_dim(flat, first_start, PANEL, 1))
    flat = flat - product(first_q, product(first_q.T, flat))
    second_lower, second_q = orthogonalize(lax.dynamic_slice_in_dim(flat, second_start, PANEL, 1))
    flat = flat - product(second_q, product(second_q.T, flat))
    result = flat * RESCALE
    zero = jnp.zeros((), jnp.int32)
    result = lax.dynamic_update_slice(result, first_q * float(L), (zero, first_start))
    result = lax.dynamic_update_slice(result, second_q * float(L), (zero, second_start))
    growth = jnp.stack([jnp.log(jnp.diagonal(first_lower)), jnp.log(jnp.diagonal(second_lower))])
    return (result.reshape(L, L, COLS), growth)
```

```python
import jax
import jax.numpy as jnp
from jax import lax
from jax.sharding import PartitionSpec as P

STEPS = 4
PANEL = 256
ENERGY = 0.5
RESCALE = 0.015625

Z, CORE, X, Y = 8, 2, 4, 8


def x_shift(value, k):
    return lax.ppermute(value, "col", [(x * Y + y, ((x + k) % X) * Y + y) for x in range(X) for y in range(Y)])


def y_shift(value, k):
    return lax.ppermute(value, "col", [(x * Y + y, x * Y + (y + k) % Y) for x in range(X) for y in range(Y)])


def z_shift(value, k):
    return lax.ppermute(value, "site", [(z * CORE + c, ((z + k) % Z) * CORE + c) for z in range(Z) for c in range(CORE)])


def core_swap(value):
    return lax.ppermute(value, "site", [(z * CORE + c, z * CORE + 1 - c) for z in range(Z) for c in range(CORE)])


def padded_2(value):
    size, length = lax.axis_size("site"), value.shape[0]
    up = [(i, (i + 1) % size) for i in range(size)]
    down = [(j, i) for i, j in up]
    before = lax.ppermute(value[length - 1 :], "site", up)
    after = lax.ppermute(value[:1], "site", down)
    return jnp.concatenate([before, value, after], axis=0)


def product(left, right):
    return jnp.dot(left, right, precision=lax.Precision.HIGHEST, preferred_element_type=jnp.float32)


def product_t(left, right):
    dims = (((0,), (0,)), ((), ()))
    return lax.dot_general(left, right, dims, precision=lax.Precision.HIGHEST, preferred_element_type=jnp.float32)


def scatter(value, shift, me, size):
    rows = value.shape[0] // size
    out = []
    for k in range(size):
        piece = lax.dynamic_slice_in_dim(value, lax.rem(me + k, size) * rows, rows, 0)
        out.append(piece if k == 0 else shift(piece, k))
    return out


def gather(value, shift, me, size):
    parts = [value if k == 0 else shift(value, k) for k in range(size)]
    parts = parts[::-1]
    double = jnp.concatenate(parts + parts[:-1], axis=0)
    rows = value.shape[0]
    return lax.dynamic_slice_in_dim(double, (size - 1 - me) * rows, rows * size, 0)


def pick(parts, index):
    out = parts[0]
    for k in range(1, len(parts)):
        out = jnp.where(index == k, parts[k], out)
    return out


def fetch_panels(flat, panels):
    col = lax.axis_index("col")
    x, y = col // Y, lax.rem(col, Y)
    quarters = scatter(flat, x_shift, x, X)
    chosen = [pick(quarters, lax.rem(x - panel // Y + X, X)) for panel in panels]
    rows = chosen[0].shape[0] // Y
    both = jnp.concatenate([c.reshape(Y, rows, PANEL) for c in chosen], axis=1).reshape(-1, PANEL)
    eighths = scatter(both, y_shift, y, Y)
    mine = [
        pick([e[n * rows : (n + 1) * rows] for e in eighths], lax.rem(y - lax.rem(panel, Y) + Y, Y))
        for n, panel in enumerate(panels)
    ]
    both = gather(jnp.concatenate(mine, axis=0), y_shift, y, Y)
    both = gather(both, x_shift, x, X)
    both = both.reshape(X * Y, len(panels), rows, PANEL)
    return [both[:, n].reshape(-1, PANEL) for n in range(len(panels))]


def sum_sites(value):
    site = lax.axis_index("site")
    z, core = site // CORE, lax.rem(site, CORE)
    half = value.shape[0] // CORE
    keep = lax.dynamic_slice_in_dim(value, core * half, half, 0)
    give = lax.dynamic_slice_in_dim(value, (1 - core) * half, half, 0)
    value = keep + core_swap(give)
    parts = scatter(value, z_shift, z, Z)
    total = parts[0]
    for part in parts[1:]:
        total = total + part
    value = gather(total, z_shift, z, Z)
    other = core_swap(value)
    return jnp.where(core == 0, jnp.concatenate([value, other]), jnp.concatenate([other, value]))


def inverse_factor(gram):
    lower = jnp.linalg.cholesky(gram)
    inverse = jax.scipy.linalg.solve_triangular(lower, jnp.eye(PANEL, dtype=jnp.float32), lower=True)
    return inverse, jnp.log(jnp.diagonal(lower))


def on_device(state_prev, state_cur, occupancy, panel_order):
    rows, side, width = state_cur.shape
    start = lax.axis_index("site") * rows
    local_mask = lax.dynamic_slice_in_dim(occupancy, start, rows, 1)
    previous, current = (state_prev, state_cur)
    for turn in range(STEPS):
        weights = local_mask[turn].astype(jnp.float32)[:, :, None]
        padded = padded_2(current)
        neighbours = padded[2:] + padded[:-2] + jnp.roll(current, 1, 1) + jnp.roll(current, -1, 1)
        previous, current = (current, weights * (ENERGY * current - neighbours - previous))
    flat = current.reshape(rows * side, width)
    first, second = panel_order[0], panel_order[1]
    a, b = fetch_panels(flat, (first, second))

    ax, bx = product_t(a, flat), product_t(b, flat)
    aa, ab, bb = product_t(a, a), product_t(a, b), product_t(b, b)
    total = sum_sites(jnp.concatenate([aa, ab, bb, ax, bx], axis=0))
    aa, ab, bb, ax, bx = [total[n * PANEL : (n + 1) * PANEL] for n in range(5)]

    inverse_1, growth_1 = inverse_factor(aa)
    cross = product(inverse_1, ab)
    inverse_2, growth_2 = inverse_factor(bb - product_t(cross, cross))
    inner_1 = product(inverse_1, ax)
    inner_2 = product(inverse_2, bx - product_t(cross, inner_1))

    col = lax.axis_index("col")
    is_first, is_second = col == first, col == second
    eye = jnp.eye(PANEL, dtype=jnp.float32) * (-float(side))
    zero = jnp.zeros_like(eye)
    inner_1 = jnp.where(is_first, eye, jnp.where(is_second, zero, inner_1 * RESCALE))
    inner_2 = jnp.where(is_first, zero, jnp.where(is_second, eye, inner_2 * RESCALE))
    weight_b = product_t(inverse_2, inner_2)
    weight_a = product_t(inverse_1, inner_1 - product(cross, weight_b))
    scale = jnp.where(jnp.logical_or(is_first, is_second), 0.0, RESCALE)
    both = jnp.concatenate([a, b], axis=1)
    weight = jnp.concatenate([weight_a, weight_b], axis=0)
    result = flat * scale - product(both, weight)
    return (result.reshape(rows, side, width), jnp.stack([growth_1, growth_2]))


def solution(mesh):
    return jax.shard_map(
        on_device,
        mesh=mesh,
        in_specs=(P("site", None, "col"), P("site", None, "col"), P(), P()),
        out_specs=(P("site", None, "col"), P()),
        check_vma=False,
    )
```

```python
import jax
import jax.numpy as jnp
from jax import lax
from jax.sharding import PartitionSpec as P

STEPS = 4
PANEL = 256
ENERGY = 0.5
RESCALE = 0.015625

SITE = ("z", "core")
COL = ("x", "y")


def exchange(value, axis):
    size = lax.axis_size(axis)
    out = lax.all_to_all(value, axis, 0, 0, tiled=True)
    return out.reshape((size, value.shape[0] // size) + value.shape[1:])


def gather(value, axis):
    size = lax.axis_size(axis)
    copies = jnp.broadcast_to(value[None], (size,) + value.shape)
    return lax.all_to_all(copies.reshape((-1,) + value.shape[1:]), axis, 0, 0, tiled=True)


def padded_2(value):
    size, length = lax.axis_size(SITE), value.shape[0]
    up = [(i, (i + 1) % size) for i in range(size)]
    down = [(j, i) for i, j in up]
    before = lax.ppermute(value[length - 1 :], SITE, up)
    after = lax.ppermute(value[:1], SITE, down)
    return jnp.concatenate([before, value, after], axis=0)


def product(left, right):
    return jnp.dot(left, right, precision=lax.Precision.HIGHEST, preferred_element_type=jnp.float32)


def product_t(left, right):
    dims = (((0,), (0,)), ((), ()))
    return lax.dot_general(left, right, dims, precision=lax.Precision.HIGHEST, preferred_element_type=jnp.float32)


def fetch_panels(flat, panels):
    ny = lax.axis_size("y")
    received = exchange(flat, "x")
    quarters = [lax.dynamic_index_in_dim(received, panel // ny, 0, False) for panel in panels]
    rows = quarters[0].shape[0] // ny
    both = jnp.concatenate([q.reshape(ny, rows, PANEL) for q in quarters], axis=1)
    received = exchange(both.reshape(-1, PANEL), "y").reshape(ny, len(panels), rows, PANEL)
    mine = [lax.dynamic_index_in_dim(received[:, n], lax.rem(panel, ny), 0, False) for n, panel in enumerate(panels)]
    both = gather(gather(jnp.concatenate(mine, axis=0), "y"), "x")
    both = both.reshape(-1, len(panels), rows, PANEL)
    return [both[:, n].reshape(-1, PANEL) for n in range(len(panels))]


def sum_sites(value):
    value = exchange(value, "core").sum(axis=0)
    value = exchange(value, "z").sum(axis=0)
    return lax.all_gather(gather(value, "z"), "core", axis=0, tiled=True)


def inverse_factor(gram):
    lower = jnp.linalg.cholesky(gram)
    inverse = jax.scipy.linalg.solve_triangular(lower, jnp.eye(PANEL, dtype=jnp.float32), lower=True)
    return inverse, jnp.log(jnp.diagonal(lower))


def on_device(state_prev, state_cur, occupancy, panel_order):
    rows, side, width = state_cur.shape
    start = lax.axis_index(SITE) * rows
    local_mask = lax.dynamic_slice_in_dim(occupancy, start, rows, 1)
    previous, current = (state_prev, state_cur)
    for turn in range(STEPS):
        weights = local_mask[turn].astype(jnp.float32)[:, :, None]
        padded = padded_2(current)
        neighbours = padded[2:] + padded[:-2] + jnp.roll(current, 1, 1) + jnp.roll(current, -1, 1)
        previous, current = (current, weights * (ENERGY * current - neighbours - previous))
    flat = current.reshape(rows * side, width)
    first, second = panel_order[0], panel_order[1]
    a, b = fetch_panels(flat, (first, second))

    aa, ab, bb = product_t(a, a), product_t(a, b), product_t(b, b)
    gram = sum_sites(jnp.concatenate([aa, ab, bb], axis=0))
    aa, ab, bb = [gram[n * PANEL : (n + 1) * PANEL] for n in range(3)]
    a_late, b_late, gram = lax.optimization_barrier((a, b, gram))
    inner = sum_sites(jnp.concatenate([product_t(a_late, flat), product_t(b_late, flat)], axis=0))
    ax, bx = inner[:PANEL], inner[PANEL:]

    inverse_1, growth_1 = inverse_factor(aa)
    cross = product(inverse_1, ab)
    inverse_2, growth_2 = inverse_factor(bb - product_t(cross, cross))
    inner_1 = product(inverse_1, ax)
    inner_2 = product(inverse_2, bx - product_t(cross, inner_1))

    col = lax.axis_index(COL)
    is_first, is_second = col == first, col == second
    eye = jnp.eye(PANEL, dtype=jnp.float32) * (-float(side))
    zero = jnp.zeros_like(eye)
    inner_1 = jnp.where(is_first, eye, jnp.where(is_second, zero, inner_1 * RESCALE))
    inner_2 = jnp.where(is_first, zero, jnp.where(is_second, eye, inner_2 * RESCALE))
    weight_b = product_t(inverse_2, inner_2)
    weight_a = product_t(inverse_1, inner_1 - product(cross, weight_b))
    scale = jnp.where(jnp.logical_or(is_first, is_second), 0.0, RESCALE)
    both = jnp.concatenate([a, b], axis=1)
    weight = jnp.concatenate([weight_a, weight_b], axis=0)
    result = flat * scale - product(both, weight)
    return (result.reshape(rows, side, width), jnp.stack([growth_1, growth_2]))


def solution(mesh):
    mesh = jax.sharding.Mesh(mesh.devices.reshape(8, 2, 4, 8), SITE + COL)
    return jax.shard_map(
        on_device,
        mesh=mesh,
        in_specs=(P(SITE, None, COL), P(SITE, None, COL), P(), P()),
        out_specs=(P(SITE, None, COL), P()),
        check_vma=False,
    )
```

```python
import jax
import jax.numpy as jnp
from jax import lax
from jax.experimental import pallas as pl
from jax.experimental.pallas import tpu as pltpu
from jax.sharding import PartitionSpec as P

STEPS = 4
PANEL = 256
ENERGY = 0.5
RESCALE = 0.015625
BLOCK = 8

SITE = ("z", "core")
COL = ("x", "y")


def exchange(value, axis):
    size = lax.axis_size(axis)
    out = lax.all_to_all(value, axis, 0, 0, tiled=True)
    return out.reshape((size, value.shape[0] // size) + value.shape[1:])


def gather(value, axis):
    size = lax.axis_size(axis)
    copies = jnp.broadcast_to(value[None], (size,) + value.shape)
    return lax.all_to_all(copies.reshape((-1,) + value.shape[1:]), axis, 0, 0, tiled=True)


def padded_2(value):
    size, length = lax.axis_size(SITE), value.shape[0]
    up = [(i, (i + 1) % size) for i in range(size)]
    down = [(j, i) for i, j in up]
    before = lax.ppermute(value[length - 1 :], SITE, up)
    after = lax.ppermute(value[:1], SITE, down)
    return jnp.concatenate([before, value, after], axis=0)


def product(left, right):
    return jnp.dot(left, right, precision=lax.Precision.HIGHEST, preferred_element_type=jnp.float32)


def product_t(left, right):
    dims = (((0,), (0,)), ((), ()))
    return lax.dot_general(left, right, dims, precision=lax.Precision.HIGHEST, preferred_element_type=jnp.float32)


def fetch_panels(flat, panels):
    ny = lax.axis_size("y")
    received = exchange(flat, "x")
    quarters = [lax.dynamic_index_in_dim(received, panel // ny, 0, False) for panel in panels]
    rows = quarters[0].shape[0] // ny
    both = jnp.concatenate([q.reshape(ny, rows, PANEL) for q in quarters], axis=1)
    received = exchange(both.reshape(-1, PANEL), "y").reshape(ny, len(panels), rows, PANEL)
    mine = [lax.dynamic_index_in_dim(received[:, n], lax.rem(panel, ny), 0, False) for n, panel in enumerate(panels)]
    both = gather(gather(jnp.concatenate(mine, axis=0), "y"), "x")
    both = both.reshape(-1, len(panels), rows, PANEL)
    return [both[:, n].reshape(-1, PANEL) for n in range(len(panels))]


def sum_sites(value):
    value = exchange(value, "core").sum(axis=0)
    value = exchange(value, "z").sum(axis=0)
    return lax.all_gather(gather(value, "z"), "core", axis=0, tiled=True)


def split3(x):
    high = x.astype(jnp.bfloat16).astype(jnp.float32)
    rest = x - high
    mid = rest.astype(jnp.bfloat16).astype(jnp.float32)
    return high, mid, rest - mid


def outer(left, right):
    a, b, c = split3(left)
    d, e, f = split3(right)
    lhs = jnp.concatenate([a, a, b, a, c, b], axis=0).astype(jnp.bfloat16)
    rhs = jnp.concatenate([d, e, d, f, d, e], axis=0).astype(jnp.bfloat16)
    return lax.dot_general(lhs, rhs, (((0,), (0,)), ((), ())), preferred_element_type=jnp.float32)


def factor_kernel(gram_ref, out_ref):
    n = gram_ref.shape[0]
    lane = lax.broadcasted_iota(jnp.int32, (BLOCK, n), 1)
    sub = lax.broadcasted_iota(jnp.int32, (BLOCK, n), 0)
    sub1 = lax.broadcasted_iota(jnp.int32, (BLOCK, 128), 0)
    lane_all = lax.broadcasted_iota(jnp.int32, (n, n), 1)
    out_ref[...] = gram_ref[...]

    def step(j, _):
        r = pl.multiple_of(j * BLOCK, BLOCK)
        panel = out_ref[pl.ds(r, BLOCK), :]
        entry = {}
        for m in range(BLOCK):
            column = jnp.sum(jnp.where(lane == r + m, panel, 0.0), axis=1, keepdims=True)
            column = jnp.broadcast_to(column, (BLOCK, 128))
            for i in range(m, BLOCK):
                entry[i, m] = jnp.broadcast_to(column[i : i + 1], (BLOCK, 128))
        inv = {}
        for k in range(BLOCK):
            root = lax.rsqrt(entry[k, k])
            for i in range(k + 1, BLOCK):
                entry[i, k] = entry[i, k] * root
            for m in range(k + 1, BLOCK):
                for i in range(m, BLOCK):
                    entry[i, m] = entry[i, m] - entry[i, k] * entry[m, k]
            for c in range(k):
                acc = entry[k, c] * inv[c, c]
                for m in range(c + 1, k):
                    acc = acc + entry[k, m] * inv[m, c]
                inv[k, c] = -root * acc
            inv[k, k] = root
        inside = jnp.logical_and(lane >= r, lane < r + BLOCK)
        panel = jnp.where(inside, jnp.where(lane - r == sub, 1.0, 0.0), panel)
        new = None
        for k in range(BLOCK):
            column = jnp.zeros((BLOCK, 128), jnp.float32)
            for i in range(k, BLOCK):
                column = jnp.where(sub1 == i, inv[i, k], column)
            column = jnp.concatenate([column] * (n // 128), axis=1)
            term = column * jnp.broadcast_to(panel[k : k + 1], (BLOCK, n))
            new = term if new is None else new + term
        ahead = jnp.where(lane >= r + BLOCK, new, 0.0)
        inside = jnp.logical_and(lane_all >= r, lane_all < r + BLOCK)
        out_ref[...] = jnp.where(inside, 0.0, out_ref[...]) - outer(ahead, new)
        out_ref[pl.ds(r, BLOCK), :] = new
        return 0

    lax.fori_loop(0, n // BLOCK, step, 0)


def factor(gram):
    inverse = pl.pallas_call(
        factor_kernel,
        out_shape=jax.ShapeDtypeStruct(gram.shape, jnp.float32),
        in_specs=[pl.BlockSpec(memory_space=pltpu.VMEM)],
        out_specs=pl.BlockSpec(memory_space=pltpu.VMEM),
        cost_estimate=pl.CostEstimate(flops=16_000_000_000, bytes_accessed=524288, transcendentals=256),
    )(gram)
    eye = jnp.eye(gram.shape[0], dtype=bool)
    return inverse, -jnp.log(jnp.sum(jnp.where(eye, inverse, 0.0), axis=0))


def on_device(state_prev, state_cur, occupancy, panel_order):
    rows, side, width = state_cur.shape
    start = lax.axis_index(SITE) * rows
    local_mask = lax.dynamic_slice_in_dim(occupancy, start, rows, 1)
    previous, current = (state_prev, state_cur)
    for turn in range(STEPS):
        weights = local_mask[turn].astype(jnp.float32)[:, :, None]
        padded = padded_2(current)
        neighbours = padded[2:] + padded[:-2] + jnp.roll(current, 1, 1) + jnp.roll(current, -1, 1)
        previous, current = (current, weights * (ENERGY * current - neighbours - previous))
    flat = current.reshape(rows * side, width)
    first, second = panel_order[0], panel_order[1]
    a, b = fetch_panels(flat, (first, second))

    aa, ab, bb = product_t(a, a), product_t(a, b), product_t(b, b)
    gram = sum_sites(jnp.concatenate([aa, ab, bb], axis=0))
    aa, ab, bb = [gram[n * PANEL : (n + 1) * PANEL] for n in range(3)]
    a_late, b_late, gram = lax.optimization_barrier((a, b, gram))
    inner = sum_sites(jnp.concatenate([product_t(a_late, flat), product_t(b_late, flat)], axis=0))
    ax, bx = inner[:PANEL], inner[PANEL:]

    inverse_1, growth_1 = factor(aa)
    cross = product(inverse_1, ab)
    inverse_2, growth_2 = factor(bb - product_t(cross, cross))
    inner_1 = product(inverse_1, ax)
    inner_2 = product(inverse_2, bx - product_t(cross, inner_1))

    col = lax.axis_index(COL)
    is_first, is_second = col == first, col == second
    eye = jnp.eye(PANEL, dtype=jnp.float32) * (-float(side))
    zero = jnp.zeros_like(eye)
    inner_1 = jnp.where(is_first, eye, jnp.where(is_second, zero, inner_1 * RESCALE))
    inner_2 = jnp.where(is_first, zero, jnp.where(is_second, eye, inner_2 * RESCALE))
    weight_b = product_t(inverse_2, inner_2)
    weight_a = product_t(inverse_1, inner_1 - product(cross, weight_b))
    scale = jnp.where(jnp.logical_or(is_first, is_second), 0.0, RESCALE)
    both = jnp.concatenate([a, b], axis=1)
    weight = jnp.concatenate([weight_a, weight_b], axis=0)
    result = flat * scale - product(both, weight)
    return (result.reshape(rows, side, width), jnp.stack([growth_1, growth_2]))


def solution(mesh):
    mesh = jax.sharding.Mesh(mesh.devices.reshape(8, 2, 4, 8), SITE + COL)
    return jax.shard_map(
        on_device,
        mesh=mesh,
        in_specs=(P(SITE, None, COL), P(SITE, None, COL), P(), P()),
        out_specs=(P(SITE, None, COL), P()),
        check_vma=False,
    )
```

```python
import jax
import jax.numpy as jnp
from jax import lax
from jax.experimental import pallas as pl
from jax.experimental.pallas import tpu as pltpu
from jax.sharding import PartitionSpec as P

STEPS = 4
PANEL = 256
ENERGY = 0.5
RESCALE = 0.015625
BLOCK = 8

SITE = ("z", "core")
COL = ("x", "y")


def exchange(value, axis):
    size = lax.axis_size(axis)
    out = lax.all_to_all(value, axis, 0, 0, tiled=True)
    return out.reshape((size, value.shape[0] // size) + value.shape[1:])


def gather(value, axis):
    size = lax.axis_size(axis)
    copies = jnp.broadcast_to(value[None], (size,) + value.shape)
    return lax.all_to_all(copies.reshape((-1,) + value.shape[1:]), axis, 0, 0, tiled=True)


def padded_2(value):
    size, length = lax.axis_size(SITE), value.shape[0]
    up = [(i, (i + 1) % size) for i in range(size)]
    down = [(j, i) for i, j in up]
    before = lax.ppermute(value[length - 1 :], SITE, up)
    after = lax.ppermute(value[:1], SITE, down)
    return jnp.concatenate([before, value, after], axis=0)


def product(left, right):
    return jnp.dot(left, right, precision=lax.Precision.HIGHEST, preferred_element_type=jnp.float32)


def product_t(left, right):
    dims = (((0,), (0,)), ((), ()))
    return lax.dot_general(left, right, dims, precision=lax.Precision.HIGHEST, preferred_element_type=jnp.float32)


def fetch_panels(flat, panels):
    received = exchange(flat, COL)
    mine = jnp.concatenate([lax.dynamic_index_in_dim(received, panel, 0, False) for panel in panels], axis=0)
    both = gather(gather(mine, "y"), "x")
    both = both.reshape(-1, len(panels), received.shape[1], PANEL)
    return [both[:, n].reshape(-1, PANEL) for n in range(len(panels))]


def split3(x):
    high = x.astype(jnp.bfloat16).astype(jnp.float32)
    rest = x - high
    mid = rest.astype(jnp.bfloat16).astype(jnp.float32)
    return high, mid, rest - mid


def outer(left, right):
    a, b, c = split3(left)
    d, e, f = split3(right)
    lhs = jnp.concatenate([a, a, b, a, c, b], axis=0).astype(jnp.bfloat16)
    rhs = jnp.concatenate([d, e, d, f, d, e], axis=0).astype(jnp.bfloat16)
    return lax.dot_general(lhs, rhs, (((0,), (0,)), ((), ())), preferred_element_type=jnp.float32)


def factor_kernel(gram_ref, out_ref):
    n = gram_ref.shape[0]
    lane = lax.broadcasted_iota(jnp.int32, (BLOCK, n), 1)
    sub = lax.broadcasted_iota(jnp.int32, (BLOCK, n), 0)
    sub1 = lax.broadcasted_iota(jnp.int32, (BLOCK, 128), 0)
    lane_all = lax.broadcasted_iota(jnp.int32, (n, n), 1)
    out_ref[...] = gram_ref[...]

    def step(j, _):
        r = pl.multiple_of(j * BLOCK, BLOCK)
        panel = out_ref[pl.ds(r, BLOCK), :]
        entry = {}
        for m in range(BLOCK):
            column = jnp.sum(jnp.where(lane == r + m, panel, 0.0), axis=1, keepdims=True)
            column = jnp.broadcast_to(column, (BLOCK, 128))
            for i in range(m, BLOCK):
                entry[i, m] = jnp.broadcast_to(column[i : i + 1], (BLOCK, 128))
        inv = {}
        for k in range(BLOCK):
            root = lax.rsqrt(entry[k, k])
            for i in range(k + 1, BLOCK):
                entry[i, k] = entry[i, k] * root
            for m in range(k + 1, BLOCK):
                for i in range(m, BLOCK):
                    entry[i, m] = entry[i, m] - entry[i, k] * entry[m, k]
            for c in range(k):
                acc = entry[k, c] * inv[c, c]
                for m in range(c + 1, k):
                    acc = acc + entry[k, m] * inv[m, c]
                inv[k, c] = -root * acc
            inv[k, k] = root
        inside = jnp.logical_and(lane >= r, lane < r + BLOCK)
        panel = jnp.where(inside, jnp.where(lane - r == sub, 1.0, 0.0), panel)
        new = None
        for k in range(BLOCK):
            column = jnp.zeros((BLOCK, 128), jnp.float32)
            for i in range(k, BLOCK):
                column = jnp.where(sub1 == i, inv[i, k], column)
            column = jnp.concatenate([column] * (n // 128), axis=1)
            term = column * jnp.broadcast_to(panel[k : k + 1], (BLOCK, n))
            new = term if new is None else new + term
        ahead = jnp.where(lane >= r + BLOCK, new, 0.0)
        inside = jnp.logical_and(lane_all >= r, lane_all < r + BLOCK)
        out_ref[...] = jnp.where(inside, 0.0, out_ref[...]) - outer(ahead, new)
        out_ref[pl.ds(r, BLOCK), :] = new
        return 0

    lax.fori_loop(0, n // BLOCK, step, 0)


def factor(gram):
    return pl.pallas_call(
        factor_kernel,
        out_shape=jax.ShapeDtypeStruct(gram.shape, jnp.float32),
        in_specs=[pl.BlockSpec(memory_space=pltpu.VMEM)],
        out_specs=pl.BlockSpec(memory_space=pltpu.VMEM),
        cost_estimate=pl.CostEstimate(flops=16_000_000_000, bytes_accessed=524288, transcendentals=256),
    )(gram)


def growth(inverse):
    eye = jnp.eye(inverse.shape[0], dtype=bool)
    return -jnp.log(jnp.sum(jnp.where(eye, inverse, 0.0), axis=0))


def on_device(state_prev, state_cur, occupancy, panel_order):
    rows, side, width = state_cur.shape
    start = lax.axis_index(SITE) * rows
    local_mask = lax.dynamic_slice_in_dim(occupancy, start, rows, 1)
    previous, current = (state_prev, state_cur)
    for turn in range(STEPS):
        weights = local_mask[turn].astype(jnp.float32)[:, :, None]
        padded = padded_2(current)
        neighbours = padded[2:] + padded[:-2] + jnp.roll(current, 1, 1) + jnp.roll(current, -1, 1)
        previous, current = (current, weights * (ENERGY * current - neighbours - previous))
    flat = current.reshape(rows * side, width)
    first, second = panel_order[0], panel_order[1]
    a, b = fetch_panels(flat, (first, second))

    half = PANEL // 2
    aa, ab, bb = product_t(a, a), product_t(a, b), product_t(b, b)
    corners = jnp.concatenate([aa[half:, half:], bb[half:, half:]], axis=1)
    gram = jnp.concatenate([aa[:half], bb[:half], corners, ab], axis=0)
    gram = exchange(gram, "core").sum(axis=0)
    a_late, b_late, gram = lax.optimization_barrier((a, b, gram))
    inner = jnp.concatenate([product_t(a_late, flat), product_t(b_late, flat)], axis=0)
    gram = gather(exchange(gram, "z").sum(axis=0), "z")
    inner = exchange(inner, "core").sum(axis=0)
    inner, gram = lax.optimization_barrier((inner, lax.all_gather(gram, "core", axis=0, tiled=True)))
    inner = exchange(inner, "z").sum(axis=0)
    corners, ab = gram[PANEL : PANEL + half], gram[PANEL + half :]
    unread = jnp.zeros((half, half), jnp.float32)
    aa = jnp.concatenate([gram[:half], jnp.concatenate([unread, corners[:, :half]], axis=1)], axis=0)
    bb = jnp.concatenate([gram[half:PANEL], jnp.concatenate([unread, corners[:, half:]], axis=1)], axis=0)

    inner, inverse_1 = lax.optimization_barrier((inner, factor(aa)))
    cross = product(inverse_1, ab)
    inner, inverse_2 = lax.optimization_barrier((gather(inner, "z"), factor(bb - product_t(cross, cross))))
    inner = lax.all_gather(inner, "core", axis=0, tiled=True)
    ax, bx = inner[:PANEL], inner[PANEL:]
    inner_1 = product(inverse_1, ax)
    inner_2 = product(inverse_2, bx - product_t(cross, inner_1))

    col = lax.axis_index(COL)
    is_first, is_second = col == first, col == second
    eye = jnp.eye(PANEL, dtype=jnp.float32) * (-float(side))
    zero = jnp.zeros_like(eye)
    inner_1 = jnp.where(is_first, eye, jnp.where(is_second, zero, inner_1 * RESCALE))
    inner_2 = jnp.where(is_first, zero, jnp.where(is_second, eye, inner_2 * RESCALE))
    weight_b = product_t(inverse_2, inner_2)
    weight_a = product_t(inverse_1, inner_1 - product(cross, weight_b))
    scale = jnp.where(jnp.logical_or(is_first, is_second), 0.0, RESCALE)
    both = jnp.concatenate([a, b], axis=1)
    weight = jnp.concatenate([weight_a, weight_b], axis=0)
    result = flat * scale - product(both, weight)
    return (result.reshape(rows, side, width), jnp.stack([growth(inverse_1), growth(inverse_2)]))


def solution(mesh):
    mesh = jax.sharding.Mesh(mesh.devices.reshape(8, 2, 4, 8), SITE + COL)
    return jax.shard_map(
        on_device,
        mesh=mesh,
        in_specs=(P(SITE, None, COL), P(SITE, None, COL), P(), P()),
        out_specs=(P(SITE, None, COL), P()),
        check_vma=False,
    )
```

```python
import jax
import jax.numpy as jnp
from jax import lax
from jax.experimental import pallas as pl
from jax.experimental.pallas import tpu as pltpu
from jax.sharding import PartitionSpec as P

STEPS = 4
PANEL = 256
ENERGY = 0.5
RESCALE = 0.015625
BLOCK = 8

SITE = ("z", "core")
COL = ("x", "y")


def exchange(value, axis):
    size = lax.axis_size(axis)
    out = lax.all_to_all(value, axis, 0, 0, tiled=True)
    return out.reshape((size, value.shape[0] // size) + value.shape[1:])


def gather(value, axis):
    size = lax.axis_size(axis)
    copies = jnp.broadcast_to(value[None], (size,) + value.shape)
    return lax.all_to_all(copies.reshape((-1,) + value.shape[1:]), axis, 0, 0, tiled=True)


def halos(previous, current):
    size, length = lax.axis_size(SITE), current.shape[0]
    up = [(i, (i + 1) % size) for i in range(size)]
    down = [(j, i) for i, j in up]
    last = jnp.concatenate([previous[length - STEPS + 1 :], current[length - STEPS :]], axis=0)
    leading = jnp.concatenate([previous[: STEPS - 1], current[:STEPS]], axis=0)
    return lax.ppermute(last, SITE, up), lax.ppermute(leading, SITE, down)


def window_kernel(previous_ref, current_ref, before_ref, after_ref, weight_ref, out_ref, even, odd):
    rows = current_ref.shape[0]
    depth = STEPS
    even[pl.ds(0, depth)] = before_ref[pl.ds(depth - 1, depth)]
    even[pl.ds(depth, rows)] = current_ref[...]
    even[pl.ds(depth + rows, depth)] = after_ref[pl.ds(depth - 1, depth)]
    odd[pl.ds(1, depth - 1)] = before_ref[pl.ds(0, depth - 1)]
    odd[pl.ds(depth, rows)] = previous_ref[...]
    odd[pl.ds(depth + rows, depth - 1)] = after_ref[pl.ds(0, depth - 1)]
    for turn in range(STEPS):
        current, previous = (even, odd) if turn % 2 == 0 else (odd, even)
        last = turn == STEPS - 1

        for row in range(turn + 1, rows + 2 * depth - 1 - turn):
            here = current[row]
            neighbours = current[row + 1] + current[row - 1] + pltpu.roll(here, 1, 0) + pltpu.roll(here, here.shape[0] - 1, 0)
            value = weight_ref[turn, :, row : row + 1] * (ENERGY * here - neighbours - previous[row])
            if last:
                out_ref[row - depth] = value
            else:
                previous[row] = value


def window(previous, current, occupancy):
    rows, side, width = current.shape
    before, after = halos(previous, current)
    start = lax.axis_index(SITE) * rows
    around = jnp.concatenate([occupancy[:, side - STEPS :], occupancy, occupancy[:, :STEPS]], axis=1)
    weights = lax.dynamic_slice_in_dim(around, start, rows + 2 * STEPS, 1).astype(jnp.float32).transpose(0, 2, 1)
    slab = pltpu.VMEM((rows + 2 * STEPS, side, width), jnp.float32)
    return pl.pallas_call(
        window_kernel,
        out_shape=jax.ShapeDtypeStruct(current.shape, jnp.float32),
        in_specs=[pl.BlockSpec(memory_space=pltpu.VMEM)] * 5,
        out_specs=pl.BlockSpec(memory_space=pltpu.VMEM),
        scratch_shapes=[slab, slab],
        compiler_params=pltpu.CompilerParams(vmem_limit_bytes=32 * 1024 * 1024),
        cost_estimate=pl.CostEstimate(flops=12_000_000, bytes_accessed=6_000_000, transcendentals=0),
    )(previous, current, before, after, weights)


def core_sum(value):
    core, half = lax.axis_index("core"), value.shape[0] // 2
    give = lax.dynamic_slice_in_dim(value, (1 - core) * half, half, 0)
    keep = lax.dynamic_slice_in_dim(value, core * half, half, 0)
    return keep + lax.ppermute(give, "core", [(0, 1), (1, 0)])


def product(left, right):
    return jnp.dot(left, right, precision=lax.Precision.HIGHEST, preferred_element_type=jnp.float32)


def product_t(left, right):
    dims = (((0,), (0,)), ((), ()))
    return lax.dot_general(left, right, dims, precision=lax.Precision.HIGHEST, preferred_element_type=jnp.float32)


def fetch_panels(flat, panels):
    received = exchange(flat, COL)
    mine = jnp.concatenate([lax.dynamic_index_in_dim(received, panel, 0, False) for panel in panels], axis=0)
    both = gather(gather(mine, "y"), "x")
    both = both.reshape(-1, len(panels), received.shape[1], PANEL)
    return [both[:, n].reshape(-1, PANEL) for n in range(len(panels))]


def split3(x):
    high = x.astype(jnp.bfloat16).astype(jnp.float32)
    rest = x - high
    mid = rest.astype(jnp.bfloat16).astype(jnp.float32)
    return high, mid, rest - mid


def outer(left, right):
    a, b, c = split3(left)
    d, e, f = split3(right)
    lhs = jnp.concatenate([a, a, b, a, c, b], axis=0).astype(jnp.bfloat16)
    rhs = jnp.concatenate([d, e, d, f, d, e], axis=0).astype(jnp.bfloat16)
    return lax.dot_general(lhs, rhs, (((0,), (0,)), ((), ())), preferred_element_type=jnp.float32)


def factor_kernel(gram_ref, out_ref):
    n = gram_ref.shape[0]
    lane = lax.broadcasted_iota(jnp.int32, (BLOCK, n), 1)
    sub = lax.broadcasted_iota(jnp.int32, (BLOCK, n), 0)
    sub1 = lax.broadcasted_iota(jnp.int32, (BLOCK, 128), 0)
    lane_all = lax.broadcasted_iota(jnp.int32, (n, n), 1)
    out_ref[...] = gram_ref[...]

    def step(j, _):
        r = pl.multiple_of(j * BLOCK, BLOCK)
        panel = out_ref[pl.ds(r, BLOCK), :]
        entry = {}
        for m in range(BLOCK):
            column = jnp.sum(jnp.where(lane == r + m, panel, 0.0), axis=1, keepdims=True)
            column = jnp.broadcast_to(column, (BLOCK, 128))
            for i in range(m, BLOCK):
                entry[i, m] = jnp.broadcast_to(column[i : i + 1], (BLOCK, 128))
        inv = {}
        for k in range(BLOCK):
            root = lax.rsqrt(entry[k, k])
            for i in range(k + 1, BLOCK):
                entry[i, k] = entry[i, k] * root
            for m in range(k + 1, BLOCK):
                for i in range(m, BLOCK):
                    entry[i, m] = entry[i, m] - entry[i, k] * entry[m, k]
            for c in range(k):
                acc = entry[k, c] * inv[c, c]
                for m in range(c + 1, k):
                    acc = acc + entry[k, m] * inv[m, c]
                inv[k, c] = -root * acc
            inv[k, k] = root
        inside = jnp.logical_and(lane >= r, lane < r + BLOCK)
        panel = jnp.where(inside, jnp.where(lane - r == sub, 1.0, 0.0), panel)
        new = None
        for k in range(BLOCK):
            column = jnp.zeros((BLOCK, 128), jnp.float32)
            for i in range(k, BLOCK):
                column = jnp.where(sub1 == i, inv[i, k], column)
            column = jnp.concatenate([column] * (n // 128), axis=1)
            term = column * jnp.broadcast_to(panel[k : k + 1], (BLOCK, n))
            new = term if new is None else new + term
        ahead = jnp.where(lane >= r + BLOCK, new, 0.0)
        inside = jnp.logical_and(lane_all >= r, lane_all < r + BLOCK)
        out_ref[...] = jnp.where(inside, 0.0, out_ref[...]) - outer(ahead, new)
        out_ref[pl.ds(r, BLOCK), :] = new
        return 0

    lax.fori_loop(0, n // BLOCK, step, 0)


def factor(gram):
    return pl.pallas_call(
        factor_kernel,
        out_shape=jax.ShapeDtypeStruct(gram.shape, jnp.float32),
        in_specs=[pl.BlockSpec(memory_space=pltpu.VMEM)],
        out_specs=pl.BlockSpec(memory_space=pltpu.VMEM),
        cost_estimate=pl.CostEstimate(flops=16_000_000_000, bytes_accessed=524288, transcendentals=256),
    )(gram)


def growth(inverse):
    eye = jnp.eye(inverse.shape[0], dtype=bool)
    return -jnp.log(jnp.sum(jnp.where(eye, inverse, 0.0), axis=0))


def on_device(state_prev, state_cur, occupancy, panel_order):
    rows, side, width = state_cur.shape
    current = window(state_prev, state_cur, occupancy)
    flat = current.reshape(rows * side, width)
    first, second = panel_order[0], panel_order[1]
    a, b = fetch_panels(flat, (first, second))

    half = PANEL // 2
    aa, ab, bb = product_t(a, a), product_t(a, b), product_t(b, b)
    corners = jnp.concatenate([aa[half:, half:], bb[half:, half:]], axis=1)
    gram = jnp.concatenate([aa[:half], bb[:half], corners, ab], axis=0)
    gram = exchange(gram, "core").sum(axis=0)
    a_late, b_late, gram = lax.optimization_barrier((a, b, gram))
    inner = jnp.concatenate([product_t(a_late, flat), product_t(b_late, flat)], axis=0)
    gram = gather(exchange(gram, "z").sum(axis=0), "z")
    inner = core_sum(inner)
    inner, gram = lax.optimization_barrier((inner, lax.all_gather(gram, "core", axis=0, tiled=True)))
    inner = exchange(inner, "z").sum(axis=0)
    corners, ab = gram[PANEL : PANEL + half], gram[PANEL + half :]
    unread = jnp.zeros((half, half), jnp.float32)
    aa = jnp.concatenate([gram[:half], jnp.concatenate([unread, corners[:, :half]], axis=1)], axis=0)
    bb = jnp.concatenate([gram[half:PANEL], jnp.concatenate([unread, corners[:, half:]], axis=1)], axis=0)

    inner, inverse_1 = lax.optimization_barrier((inner, factor(aa)))
    cross = product(inverse_1, ab)
    inner, inverse_2 = lax.optimization_barrier((gather(inner, "z"), factor(bb - product_t(cross, cross))))
    inner = lax.all_gather(inner, "core", axis=0, tiled=True)
    ax, bx = inner[:PANEL], inner[PANEL:]
    inner_1 = product(inverse_1, ax)
    inner_2 = product(inverse_2, bx - product_t(cross, inner_1))

    col = lax.axis_index(COL)
    is_first, is_second = col == first, col == second
    eye = jnp.eye(PANEL, dtype=jnp.float32) * (-float(side))
    zero = jnp.zeros_like(eye)
    inner_1 = jnp.where(is_first, eye, jnp.where(is_second, zero, inner_1 * RESCALE))
    inner_2 = jnp.where(is_first, zero, jnp.where(is_second, eye, inner_2 * RESCALE))
    weight_b = product_t(inverse_2, inner_2)
    weight_a = product_t(inverse_1, inner_1 - product(cross, weight_b))
    scale = jnp.where(jnp.logical_or(is_first, is_second), 0.0, RESCALE)
    both = jnp.concatenate([a, b], axis=1)
    weight = jnp.concatenate([weight_a, weight_b], axis=0)
    result = flat * scale - product(both, weight)
    return (result.reshape(rows, side, width), jnp.stack([growth(inverse_1), growth(inverse_2)]))


def solution(mesh):
    mesh = jax.sharding.Mesh(mesh.devices.reshape(8, 2, 4, 8), SITE + COL)
    return jax.shard_map(
        on_device,
        mesh=mesh,
        in_specs=(P(SITE, None, COL), P(SITE, None, COL), P(), P()),
        out_specs=(P(SITE, None, COL), P()),
        check_vma=False,
    )
```

```python
import jax
import jax.numpy as jnp
from jax import lax
from jax.experimental import pallas as pl
from jax.experimental.pallas import tpu as pltpu
from jax.sharding import PartitionSpec as P

STEPS = 4
PANEL = 256
ENERGY = 0.5
RESCALE = 0.015625
BLOCK = 8
GROUP = 4

SITE = ("z", "core")
COL = ("x", "y")


def exchange(value, axis):
    size = lax.axis_size(axis)
    out = lax.all_to_all(value, axis, 0, 0, tiled=True)
    return out.reshape((size, value.shape[0] // size) + value.shape[1:])


def gather(value, axis):
    size = lax.axis_size(axis)
    copies = jnp.broadcast_to(value[None], (size,) + value.shape)
    return lax.all_to_all(copies.reshape((-1,) + value.shape[1:]), axis, 0, 0, tiled=True)


def halos(previous, current):
    size, length = lax.axis_size(SITE), current.shape[0]
    up = [(i, (i + 1) % size) for i in range(size)]
    down = [(j, i) for i, j in up]
    last = jnp.concatenate([previous[length - STEPS + 1 :], current[length - STEPS :]], axis=0)
    leading = jnp.concatenate([previous[: STEPS - 1], current[:STEPS]], axis=0)
    return lax.ppermute(last, SITE, up), lax.ppermute(leading, SITE, down)


def window_kernel(previous_ref, current_ref, before_ref, after_ref, weight_ref, out_ref, even, odd):
    rows = current_ref.shape[0]
    depth = STEPS
    even[pl.ds(0, depth)] = before_ref[pl.ds(depth - 1, depth)]
    even[pl.ds(depth, rows)] = current_ref[...]
    even[pl.ds(depth + rows, depth)] = after_ref[pl.ds(depth - 1, depth)]
    odd[pl.ds(1, depth - 1)] = before_ref[pl.ds(0, depth - 1)]
    odd[pl.ds(depth, rows)] = previous_ref[...]
    odd[pl.ds(depth + rows, depth - 1)] = after_ref[pl.ds(0, depth - 1)]
    for turn in range(STEPS):
        current, previous = (even, odd) if turn % 2 == 0 else (odd, even)
        last = turn == STEPS - 1

        for row in range(turn + 1, rows + 2 * depth - 1 - turn):
            here = current[row]
            neighbours = current[row + 1] + current[row - 1] + pltpu.roll(here, 1, 0) + pltpu.roll(here, here.shape[0] - 1, 0)
            value = weight_ref[turn, :, row : row + 1] * (ENERGY * here - neighbours - previous[row])
            if last:
                out_ref[row - depth] = value
            else:
                previous[row] = value


def window(previous, current, occupancy):
    rows, side, width = current.shape
    before, after = halos(previous, current)
    start = lax.axis_index(SITE) * rows
    around = jnp.concatenate([occupancy[:, side - STEPS :], occupancy, occupancy[:, :STEPS]], axis=1)
    weights = lax.dynamic_slice_in_dim(around, start, rows + 2 * STEPS, 1).astype(jnp.float32).transpose(0, 2, 1)
    slab = pltpu.VMEM((rows + 2 * STEPS, side, width), jnp.float32)
    return pl.pallas_call(
        window_kernel,
        out_shape=jax.ShapeDtypeStruct(current.shape, jnp.float32),
        in_specs=[pl.BlockSpec(memory_space=pltpu.VMEM)] * 5,
        out_specs=pl.BlockSpec(memory_space=pltpu.VMEM),
        scratch_shapes=[slab, slab],
        compiler_params=pltpu.CompilerParams(vmem_limit_bytes=32 * 1024 * 1024),
        cost_estimate=pl.CostEstimate(flops=12_000_000, bytes_accessed=6_000_000, transcendentals=0),
    )(previous, current, before, after, weights)


def core_sum(value):
    core, half = lax.axis_index("core"), value.shape[0] // 2
    give = lax.dynamic_slice_in_dim(value, (1 - core) * half, half, 0)
    keep = lax.dynamic_slice_in_dim(value, core * half, half, 0)
    return keep + lax.ppermute(give, "core", [(0, 1), (1, 0)])


def product(left, right):
    return jnp.dot(left, right, precision=lax.Precision.HIGHEST, preferred_element_type=jnp.float32)


def product_t(left, right):
    dims = (((0,), (0,)), ((), ()))
    return lax.dot_general(left, right, dims, precision=lax.Precision.HIGHEST, preferred_element_type=jnp.float32)


def fetch_panels(flat, panels):
    received = exchange(flat, COL)
    mine = jnp.concatenate([lax.dynamic_index_in_dim(received, panel, 0, False) for panel in panels], axis=0)
    both = gather(gather(mine, "y"), "x")
    return both.reshape(-1, len(panels), received.shape[1], PANEL)


def split3(x):
    high = x.astype(jnp.bfloat16).astype(jnp.float32)
    rest = x - high
    mid = rest.astype(jnp.bfloat16).astype(jnp.float32)
    return high, mid, rest - mid


def outer(left, right):
    a, b, c = split3(left)
    d, e, f = split3(right)
    lhs = jnp.concatenate([a, a, b, a, c, b], axis=0).astype(jnp.bfloat16)
    rhs = jnp.concatenate([d, e, d, f, d, e], axis=0).astype(jnp.bfloat16)
    return lax.dot_general(lhs, rhs, (((0,), (0,)), ((), ())), preferred_element_type=jnp.float32)


def columns_of(rows, lane, first):
    out = []
    for m in range(BLOCK):
        column = jnp.sum(jnp.where(lane == first + m, rows, 0.0), axis=1, keepdims=True)
        out.append(jnp.broadcast_to(column, (BLOCK, 128)))
    return out


def invert_block(columns):
    entry = {}
    for m in range(BLOCK):
        for i in range(m, BLOCK):
            entry[i, m] = jnp.broadcast_to(columns[m][i : i + 1], (BLOCK, 128))
    inv = {}
    for k in range(BLOCK):
        root = lax.rsqrt(entry[k, k])
        for i in range(k + 1, BLOCK):
            entry[i, k] = entry[i, k] * root
        for m in range(k + 1, BLOCK):
            for i in range(m, BLOCK):
                entry[i, m] = entry[i, m] - entry[i, k] * entry[m, k]
        for c in range(k):
            acc = entry[k, c] * inv[c, c]
            for m in range(c + 1, k):
                acc = acc + entry[k, m] * inv[m, c]
            inv[k, c] = -root * acc
        inv[k, k] = root
    return inv


def combine(columns, rows):
    n = rows.shape[1]
    out = None
    for k in range(BLOCK):
        wide = jnp.concatenate([columns[k]] * (n // 128), axis=1)
        term = wide * jnp.broadcast_to(rows[k : k + 1], (BLOCK, n))
        out = term if out is None else out + term
    return out


def eliminate(out_ref, growth_ref):
    n = out_ref.shape[0]
    lane = lax.broadcasted_iota(jnp.int32, (BLOCK, n), 1)
    sub = lax.broadcasted_iota(jnp.int32, (BLOCK, n), 0)
    sub1 = lax.broadcasted_iota(jnp.int32, (BLOCK, 128), 0)
    lane_all = lax.broadcasted_iota(jnp.int32, (n, n), 1)
    width = GROUP * BLOCK

    def step(j, _):
        first = pl.multiple_of(j * width, width)
        end = first + width
        panels = [out_ref[pl.ds(first + g * BLOCK, BLOCK), :] for g in range(GROUP)]
        done, ahead, rest = [], [], []
        for g in range(GROUP):
            r = first + g * BLOCK
            panel = panels[g]
            inside = jnp.logical_and(lane >= r, lane < r + BLOCK)
            inv = invert_block(columns_of(panel, lane, r))
            below = [columns_of(panels[h], lane, r) for h in range(g + 1, GROUP)]
            panel = jnp.where(inside, jnp.where(lane - r == sub, 1.0, 0.0), panel)
            factor_columns = []
            for k in range(BLOCK):
                column = jnp.zeros((BLOCK, 128), jnp.float32)
                for i in range(k, BLOCK):
                    column = jnp.where(sub1 == i, inv[i, k], column)
                factor_columns.append(column)
            new = combine(factor_columns, panel)
            for h in range(g + 1, GROUP):
                source = below[h - g - 1]
                weights = []
                for k in range(BLOCK):
                    acc = inv[k, 0] * source[0]
                    for m in range(1, k + 1):
                        acc = acc + inv[k, m] * source[m]
                    weights.append(acc)
                panels[h] = jnp.where(inside, 0.0, panels[h]) - combine(weights, new)
            done.append(jnp.where(lane < r + BLOCK, new, 0.0))
            ahead.append(jnp.where(lane >= end, new, 0.0))
            rest.append(jnp.where(jnp.logical_and(lane >= r + BLOCK, lane < end), 0.0, new))
        inside = jnp.logical_and(lane_all >= first, lane_all < end)
        update = outer(jnp.concatenate(ahead, axis=0), jnp.concatenate(rest, axis=0))
        out_ref[...] = jnp.where(inside, 0.0, out_ref[...]) - update
        for g in range(GROUP):
            out_ref[pl.ds(first + g * BLOCK, BLOCK), :] = done[g]
        return 0

    lax.fori_loop(0, n // width, step, 0)
    row = lax.broadcasted_iota(jnp.int32, (n, n), 0)
    growth_ref[...] = -jnp.log(jnp.sum(jnp.where(row == lane_all, out_ref[...], 0.0), axis=0, keepdims=True))


def gram_kernel(both_ref, out_ref):
    half = PANEL // 2
    a, b = [both_ref[:, n].reshape(-1, PANEL) for n in range(2)]
    out_ref[pl.ds(0, half), :] = product_t(a[:, :half], a)
    out_ref[pl.ds(half, half), :] = product_t(b[:, :half], b)
    out_ref[pl.ds(PANEL, half), pl.ds(0, half)] = product_t(a[:, half:], a[:, half:])
    out_ref[pl.ds(PANEL, half), pl.ds(half, half)] = product_t(b[:, half:], b[:, half:])
    out_ref[pl.ds(PANEL + half, PANEL), :] = product_t(a, b)


def first_kernel(gram_ref, out_ref, growth_ref):
    half = PANEL // 2
    out_ref[pl.ds(0, half), :] = gram_ref[pl.ds(0, half), :]
    out_ref[pl.ds(half, half), pl.ds(0, half)] = jnp.zeros((half, half), jnp.float32)
    out_ref[pl.ds(half, half), pl.ds(half, half)] = gram_ref[pl.ds(PANEL, half), pl.ds(0, half)]
    eliminate(out_ref, growth_ref)


def second_kernel(gram_ref, inverse_ref, out_ref, growth_ref, cross_ref):
    half = PANEL // 2
    cross = product(inverse_ref[...], gram_ref[pl.ds(PANEL + half, PANEL), :])
    cross_ref[...] = cross
    inner = product_t(cross, cross)
    out_ref[pl.ds(0, half), :] = gram_ref[pl.ds(half, half), :] - inner[:half]
    out_ref[pl.ds(half, half), pl.ds(0, half)] = jnp.zeros((half, half), jnp.float32)
    out_ref[pl.ds(half, half), pl.ds(half, half)] = gram_ref[pl.ds(PANEL, half), pl.ds(half, half)] - inner[half:, half:]
    eliminate(out_ref, growth_ref)


def on_chip(kernel, flops, *shapes):
    vmem = pl.BlockSpec(memory_space=pltpu.VMEM)
    return lambda *args: pl.pallas_call(
        kernel,
        out_shape=[jax.ShapeDtypeStruct(shape, jnp.float32) for shape in shapes],
        in_specs=[vmem] * len(args),
        out_specs=[vmem] * len(shapes),
        compiler_params=pltpu.CompilerParams(vmem_limit_bytes=32 * 1024 * 1024),
        cost_estimate=pl.CostEstimate(flops=flops, bytes_accessed=524288, transcendentals=PANEL),
    )(*args)


def on_device(state_prev, state_cur, occupancy, panel_order):
    rows, side, width = state_cur.shape
    current = window(state_prev, state_cur, occupancy)
    flat = current.reshape(rows * side, width)
    first, second = panel_order[0], panel_order[1]
    both = fetch_panels(flat, (first, second))
    (gram,) = on_chip(gram_kernel, 4_000_000_000, (PANEL * 5 // 2, PANEL))(both)
    a, b = [both[:, n].reshape(-1, PANEL) for n in range(2)]
    gram = exchange(gram, "core").sum(axis=0)
    a_late, b_late, gram = lax.optimization_barrier((a, b, gram))
    inner = jnp.concatenate([product_t(a_late, flat), product_t(b_late, flat)], axis=0)
    gram = gather(exchange(gram, "z").sum(axis=0), "z")
    inner = core_sum(inner)
    inner, gram = lax.optimization_barrier((inner, lax.all_gather(gram, "core", axis=0, tiled=True)))
    inner = exchange(inner, "z").sum(axis=0)
    square, row = (PANEL, PANEL), (1, PANEL)
    inverse_1, growth_1 = on_chip(first_kernel, 10_000_000_000, square, row)(gram)
    inner, inverse_1 = lax.optimization_barrier((inner, inverse_1))
    inverse_2, growth_2, cross = on_chip(second_kernel, 11_000_000_000, square, row, square)(gram, inverse_1)
    inner, inverse_2 = lax.optimization_barrier((gather(inner, "z"), inverse_2))
    inner = lax.all_gather(inner, "core", axis=0, tiled=True)
    ax, bx = inner[:PANEL], inner[PANEL:]
    inner_1 = product(inverse_1, ax)
    inner_2 = product(inverse_2, bx - product_t(cross, inner_1))

    col = lax.axis_index(COL)
    is_first, is_second = col == first, col == second
    eye = jnp.eye(PANEL, dtype=jnp.float32) * (-float(side))
    zero = jnp.zeros_like(eye)
    inner_1 = jnp.where(is_first, eye, jnp.where(is_second, zero, inner_1 * RESCALE))
    inner_2 = jnp.where(is_first, zero, jnp.where(is_second, eye, inner_2 * RESCALE))
    weight_b = product_t(inverse_2, inner_2)
    weight_a = product_t(inverse_1, inner_1 - product(cross, weight_b))
    scale = jnp.where(jnp.logical_or(is_first, is_second), 0.0, RESCALE)
    both = jnp.concatenate([a, b], axis=1)
    weight = jnp.concatenate([weight_a, weight_b], axis=0)
    result = flat * scale - product(both, weight)
    return (result.reshape(rows, side, width), jnp.concatenate([growth_1, growth_2], axis=0))


def solution(mesh):
    mesh = jax.sharding.Mesh(mesh.devices.reshape(8, 2, 4, 8), SITE + COL)
    return jax.shard_map(
        on_device,
        mesh=mesh,
        in_specs=(P(SITE, None, COL), P(SITE, None, COL), P(), P()),
        out_specs=(P(SITE, None, COL), P()),
        check_vma=False,
    )
```

```python
import jax
import jax.numpy as jnp
from jax import lax
from jax.experimental import pallas as pl
from jax.experimental.pallas import tpu as pltpu
from jax.sharding import PartitionSpec as P

STEPS = 4
PANEL = 256
ENERGY = 0.5
RESCALE = 0.015625
BLOCK = 8
GROUP = 4

SITE = ("z", "core")
COL = ("x", "y")


def exchange(value, axis):
    size = lax.axis_size(axis)
    out = lax.all_to_all(value, axis, 0, 0, tiled=True)
    return out.reshape((size, value.shape[0] // size) + value.shape[1:])


def gather(value, axis):
    size = lax.axis_size(axis)
    copies = jnp.broadcast_to(value[None], (size,) + value.shape)
    return lax.all_to_all(copies.reshape((-1,) + value.shape[1:]), axis, 0, 0, tiled=True)


def edges_kernel(previous_ref, current_ref, last_ref, leading_ref, sems):
    rows, depth = current_ref.shape[0], STEPS
    copies = [
        pltpu.make_async_copy(previous_ref.at[pl.ds(rows - depth + 1, depth - 1)], last_ref.at[pl.ds(0, depth - 1)], sems.at[0]),
        pltpu.make_async_copy(current_ref.at[pl.ds(rows - depth, depth)], last_ref.at[pl.ds(depth - 1, depth)], sems.at[1]),
        pltpu.make_async_copy(previous_ref.at[pl.ds(0, depth - 1)], leading_ref.at[pl.ds(0, depth - 1)], sems.at[2]),
        pltpu.make_async_copy(current_ref.at[pl.ds(0, depth)], leading_ref.at[pl.ds(depth - 1, depth)], sems.at[3]),
    ]
    for copy in copies:
        copy.start()
    for copy in copies:
        copy.wait()


def halos(previous, current):
    size = lax.axis_size(SITE)
    up = [(i, (i + 1) % size) for i in range(size)]
    down = [(j, i) for i, j in up]
    edge = jax.ShapeDtypeStruct((2 * STEPS - 1,) + current.shape[1:], jnp.float32)
    last, leading = pl.pallas_call(
        edges_kernel,
        out_shape=[edge, edge],
        in_specs=[pl.BlockSpec(memory_space=pl.ANY)] * 2,
        out_specs=[pl.BlockSpec(memory_space=pl.ANY)] * 2,
        scratch_shapes=[pltpu.SemaphoreType.DMA((4,))],
    )(previous, current)
    return lax.ppermute(last, SITE, up), lax.ppermute(leading, SITE, down)


def window_kernel(previous_ref, current_ref, before_ref, after_ref, weight_ref, out_ref, even, odd):
    rows = current_ref.shape[0]
    depth = STEPS
    even[pl.ds(0, depth)] = before_ref[pl.ds(depth - 1, depth)]
    even[pl.ds(depth, rows)] = current_ref[...]
    even[pl.ds(depth + rows, depth)] = after_ref[pl.ds(depth - 1, depth)]
    odd[pl.ds(1, depth - 1)] = before_ref[pl.ds(0, depth - 1)]
    odd[pl.ds(depth, rows)] = previous_ref[...]
    odd[pl.ds(depth + rows, depth - 1)] = after_ref[pl.ds(0, depth - 1)]
    for turn in range(STEPS):
        current, previous = (even, odd) if turn % 2 == 0 else (odd, even)
        last = turn == STEPS - 1

        for row in range(turn + 1, rows + 2 * depth - 1 - turn):
            here = current[row]
            neighbours = current[row + 1] + current[row - 1] + pltpu.roll(here, 1, 0) + pltpu.roll(here, here.shape[0] - 1, 0)
            value = weight_ref[turn, :, row : row + 1] * (ENERGY * here - neighbours - previous[row])
            if last:
                out_ref[row - depth] = value
            else:
                previous[row] = value


def window(previous, current, occupancy):
    rows, side, width = current.shape
    before, after = halos(previous, current)
    start = lax.axis_index(SITE) * rows
    around = jnp.concatenate([occupancy[:, side - STEPS :], occupancy, occupancy[:, :STEPS]], axis=1)
    weights = lax.dynamic_slice_in_dim(around, start, rows + 2 * STEPS, 1).astype(jnp.float32).transpose(0, 2, 1)
    slab = pltpu.VMEM((rows + 2 * STEPS, side, width), jnp.float32)
    return pl.pallas_call(
        window_kernel,
        out_shape=jax.ShapeDtypeStruct(current.shape, jnp.float32),
        in_specs=[pl.BlockSpec(memory_space=pltpu.VMEM)] * 5,
        out_specs=pl.BlockSpec(memory_space=pltpu.VMEM),
        scratch_shapes=[slab, slab],
        compiler_params=pltpu.CompilerParams(vmem_limit_bytes=32 * 1024 * 1024),
        cost_estimate=pl.CostEstimate(flops=12_000_000, bytes_accessed=6_000_000, transcendentals=0),
    )(previous, current, before, after, weights)


def core_sum(value):
    core, half = lax.axis_index("core"), value.shape[0] // 2
    give = lax.dynamic_slice_in_dim(value, (1 - core) * half, half, 0)
    keep = lax.dynamic_slice_in_dim(value, core * half, half, 0)
    return keep + lax.ppermute(give, "core", [(0, 1), (1, 0)])


def product(left, right):
    return jnp.dot(left, right, precision=lax.Precision.HIGHEST, preferred_element_type=jnp.float32)


def product_t(left, right):
    dims = (((0,), (0,)), ((), ()))
    return lax.dot_general(left, right, dims, precision=lax.Precision.HIGHEST, preferred_element_type=jnp.float32)


def fetch_panels(flat, panels):
    received = exchange(flat, COL)
    mine = jnp.concatenate([lax.dynamic_index_in_dim(received, panel, 0, False) for panel in panels], axis=0)
    both = gather(gather(mine, "y"), "x")
    return both.reshape(-1, len(panels), received.shape[1], PANEL)


def split3(x):
    high = x.astype(jnp.bfloat16).astype(jnp.float32)
    rest = x - high
    mid = rest.astype(jnp.bfloat16).astype(jnp.float32)
    return high, mid, rest - mid


def outer(left, right):
    a, b, c = split3(left)
    d, e, f = split3(right)
    lhs = jnp.concatenate([a, a, b, a, c, b], axis=0).astype(jnp.bfloat16)
    rhs = jnp.concatenate([d, e, d, f, d, e], axis=0).astype(jnp.bfloat16)
    return lax.dot_general(lhs, rhs, (((0,), (0,)), ((), ())), preferred_element_type=jnp.float32)


def columns_of(rows, lane, first):
    out = []
    for m in range(BLOCK):
        column = jnp.sum(jnp.where(lane == first + m, rows, 0.0), axis=1, keepdims=True)
        out.append(jnp.broadcast_to(column, (BLOCK, 128)))
    return out


def invert_block(columns):
    entry = {}
    for m in range(BLOCK):
        for i in range(m, BLOCK):
            entry[i, m] = jnp.broadcast_to(columns[m][i : i + 1], (BLOCK, 128))
    inv = {}
    for k in range(BLOCK):
        root = lax.rsqrt(entry[k, k])
        for i in range(k + 1, BLOCK):
            entry[i, k] = entry[i, k] * root
        for m in range(k + 1, BLOCK):
            for i in range(m, BLOCK):
                entry[i, m] = entry[i, m] - entry[i, k] * entry[m, k]
        for c in range(k):
            acc = entry[k, c] * inv[c, c]
            for m in range(c + 1, k):
                acc = acc + entry[k, m] * inv[m, c]
            inv[k, c] = -root * acc
        inv[k, k] = root
    return inv


def combine(columns, rows):
    n = rows.shape[1]
    out = None
    for k in range(BLOCK):
        wide = jnp.concatenate([columns[k]] * (n // 128), axis=1)
        term = wide * jnp.broadcast_to(rows[k : k + 1], (BLOCK, n))
        out = term if out is None else out + term
    return out


def eliminate(out_ref, growth_ref):
    n = out_ref.shape[0]
    lane = lax.broadcasted_iota(jnp.int32, (BLOCK, n), 1)
    sub = lax.broadcasted_iota(jnp.int32, (BLOCK, n), 0)
    sub1 = lax.broadcasted_iota(jnp.int32, (BLOCK, 128), 0)
    lane_all = lax.broadcasted_iota(jnp.int32, (n, n), 1)
    width = GROUP * BLOCK

    def step(j, _):
        first = pl.multiple_of(j * width, width)
        end = first + width
        panels = [out_ref[pl.ds(first + g * BLOCK, BLOCK), :] for g in range(GROUP)]
        done, ahead, rest = [], [], []
        for g in range(GROUP):
            r = first + g * BLOCK
            panel = panels[g]
            inside = jnp.logical_and(lane >= r, lane < r + BLOCK)
            inv = invert_block(columns_of(panel, lane, r))
            below = [columns_of(panels[h], lane, r) for h in range(g + 1, GROUP)]
            panel = jnp.where(inside, jnp.where(lane - r == sub, 1.0, 0.0), panel)
            factor_columns = []
            for k in range(BLOCK):
                column = jnp.zeros((BLOCK, 128), jnp.float32)
                for i in range(k, BLOCK):
                    column = jnp.where(sub1 == i, inv[i, k], column)
                factor_columns.append(column)
            new = combine(factor_columns, panel)
            for h in range(g + 1, GROUP):
                source = below[h - g - 1]
                weights = []
                for k in range(BLOCK):
                    acc = inv[k, 0] * source[0]
                    for m in range(1, k + 1):
                        acc = acc + inv[k, m] * source[m]
                    weights.append(acc)
                panels[h] = jnp.where(inside, 0.0, panels[h]) - combine(weights, new)
            done.append(jnp.where(lane < r + BLOCK, new, 0.0))
            ahead.append(jnp.where(lane >= end, new, 0.0))
            rest.append(jnp.where(jnp.logical_and(lane >= r + BLOCK, lane < end), 0.0, new))
        inside = jnp.logical_and(lane_all >= first, lane_all < end)
        update = outer(jnp.concatenate(ahead, axis=0), jnp.concatenate(rest, axis=0))
        out_ref[...] = jnp.where(inside, 0.0, out_ref[...]) - update
        for g in range(GROUP):
            out_ref[pl.ds(first + g * BLOCK, BLOCK), :] = done[g]
        return 0

    lax.fori_loop(0, n // width, step, 0)
    row = lax.broadcasted_iota(jnp.int32, (n, n), 0)
    growth_ref[...] = -jnp.log(jnp.sum(jnp.where(row == lane_all, out_ref[...], 0.0), axis=0, keepdims=True))


def gram_kernel(both_ref, out_ref):
    half = PANEL // 2
    a, b = [both_ref[:, n].reshape(-1, PANEL) for n in range(2)]
    out_ref[pl.ds(0, half), :] = product_t(a[:, :half], a)
    out_ref[pl.ds(half, half), :] = product_t(b[:, :half], b)
    out_ref[pl.ds(PANEL, half), pl.ds(0, half)] = product_t(a[:, half:], a[:, half:])
    out_ref[pl.ds(PANEL, half), pl.ds(half, half)] = product_t(b[:, half:], b[:, half:])
    out_ref[pl.ds(PANEL + half, PANEL), :] = product_t(a, b)


def first_kernel(gram_ref, out_ref, growth_ref):
    half = PANEL // 2
    out_ref[pl.ds(0, half), :] = gram_ref[pl.ds(0, half), :]
    out_ref[pl.ds(half, half), pl.ds(0, half)] = jnp.zeros((half, half), jnp.float32)
    out_ref[pl.ds(half, half), pl.ds(half, half)] = gram_ref[pl.ds(PANEL, half), pl.ds(0, half)]
    eliminate(out_ref, growth_ref)


def second_kernel(gram_ref, inverse_ref, out_ref, growth_ref, cross_ref):
    half = PANEL // 2
    cross = product(inverse_ref[...], gram_ref[pl.ds(PANEL + half, PANEL), :])
    cross_ref[...] = cross
    inner = product_t(cross, cross)
    out_ref[pl.ds(0, half), :] = gram_ref[pl.ds(half, half), :] - inner[:half]
    out_ref[pl.ds(half, half), pl.ds(0, half)] = jnp.zeros((half, half), jnp.float32)
    out_ref[pl.ds(half, half), pl.ds(half, half)] = gram_ref[pl.ds(PANEL, half), pl.ds(half, half)] - inner[half:, half:]
    eliminate(out_ref, growth_ref)


def on_chip(kernel, flops, *shapes):
    vmem = pl.BlockSpec(memory_space=pltpu.VMEM)
    return lambda *args: pl.pallas_call(
        kernel,
        out_shape=[jax.ShapeDtypeStruct(shape, jnp.float32) for shape in shapes],
        in_specs=[vmem] * len(args),
        out_specs=[vmem] * len(shapes),
        compiler_params=pltpu.CompilerParams(vmem_limit_bytes=32 * 1024 * 1024),
        cost_estimate=pl.CostEstimate(flops=flops, bytes_accessed=524288, transcendentals=PANEL),
    )(*args)


def on_device(state_prev, state_cur, occupancy, panel_order):
    rows, side, width = state_cur.shape
    current = window(state_prev, state_cur, occupancy)
    flat = current.reshape(rows * side, width)
    first, second = panel_order[0], panel_order[1]
    both = fetch_panels(flat, (first, second))
    (gram,) = on_chip(gram_kernel, 4_000_000_000, (PANEL * 5 // 2, PANEL))(both)
    a, b = [both[:, n].reshape(-1, PANEL) for n in range(2)]
    gram = exchange(gram, "core").sum(axis=0)
    a_late, b_late, gram = lax.optimization_barrier((a, b, gram))
    inner = jnp.concatenate([product_t(a_late, flat), product_t(b_late, flat)], axis=0)
    gram = gather(exchange(gram, "z").sum(axis=0), "z")
    inner, gram = lax.optimization_barrier((core_sum(inner), gram))
    gram = lax.all_gather(gram, "core", axis=0, tiled=True)
    inner = exchange(inner, "z").sum(axis=0)
    square, row = (PANEL, PANEL), (1, PANEL)
    inverse_1, growth_1 = on_chip(first_kernel, 1000, square, row)(gram)
    inner, inverse_1 = lax.optimization_barrier((inner, inverse_1))
    inverse_2, growth_2, cross = on_chip(second_kernel, 1000, square, row, square)(gram, inverse_1)
    inner, inverse_2 = lax.optimization_barrier((gather(inner, "z"), inverse_2))
    inner = lax.all_gather(inner, "core", axis=0, tiled=True)
    ax, bx = inner[:PANEL], inner[PANEL:]
    inner_1 = product(inverse_1, ax)
    inner_2 = product(inverse_2, bx - product_t(cross, inner_1))

    col = lax.axis_index(COL)
    is_first, is_second = col == first, col == second
    eye = jnp.eye(PANEL, dtype=jnp.float32) * (-float(side))
    zero = jnp.zeros_like(eye)
    inner_1 = jnp.where(is_first, eye, jnp.where(is_second, zero, inner_1 * RESCALE))
    inner_2 = jnp.where(is_first, zero, jnp.where(is_second, eye, inner_2 * RESCALE))
    weight_b = product_t(inverse_2, inner_2)
    weight_a = product_t(inverse_1, inner_1 - product(cross, weight_b))
    scale = jnp.where(jnp.logical_or(is_first, is_second), 0.0, RESCALE)
    both = jnp.concatenate([a, b], axis=1)
    weight = jnp.concatenate([weight_a, weight_b], axis=0)
    result = flat * scale - product(both, weight)
    return (result.reshape(rows, side, width), jnp.concatenate([growth_1, growth_2], axis=0))


def solution(mesh):
    mesh = jax.sharding.Mesh(mesh.devices.reshape(8, 2, 4, 8), SITE + COL)
    return jax.shard_map(
        on_device,
        mesh=mesh,
        in_specs=(P(SITE, None, COL), P(SITE, None, COL), P(), P()),
        out_specs=(P(SITE, None, COL), P()),
        check_vma=False,
    )
```

```python
import jax
import jax.numpy as jnp
from jax import lax
from jax.experimental import pallas as pl
from jax.experimental.pallas import tpu as pltpu
from jax.sharding import PartitionSpec as P

STEPS = 4
PANEL = 256
ENERGY = 0.5
RESCALE = 0.015625
BLOCK = 8
GROUP = 4

SITE = ("z", "core")
COL = ("x", "y")


def exchange(value, axis):
    size = lax.axis_size(axis)
    out = lax.all_to_all(value, axis, 0, 0, tiled=True)
    return out.reshape((size, value.shape[0] // size) + value.shape[1:])


def gather(value, axis):
    size = lax.axis_size(axis)
    copies = jnp.broadcast_to(value[None], (size,) + value.shape)
    return lax.all_to_all(copies.reshape((-1,) + value.shape[1:]), axis, 0, 0, tiled=True)


def edges_kernel(previous_ref, current_ref, far_ref, near_ref, sems):
    rows, depth = current_ref.shape[0], STEPS
    core = lax.axis_index("core")
    copies = []
    for n, (side, out_ref) in enumerate(((core, far_ref), (1 - core, near_ref))):
        old = previous_ref.at[pl.ds(side * (rows - depth + 1), depth - 1)]
        new = current_ref.at[pl.ds(side * (rows - depth), depth)]
        copies.append(pltpu.make_async_copy(old, out_ref.at[pl.ds(0, depth - 1)], sems.at[2 * n]))
        copies.append(pltpu.make_async_copy(new, out_ref.at[pl.ds(depth - 1, depth)], sems.at[2 * n + 1]))
    for copy in copies:
        copy.start()
    for copy in copies:
        copy.wait()


def halos(previous, current):
    size = lax.axis_size(SITE)
    edge = jax.ShapeDtypeStruct((2 * STEPS - 1,) + current.shape[1:], jnp.float32)
    far, near = pl.pallas_call(
        edges_kernel,
        out_shape=[edge, edge],
        in_specs=[pl.BlockSpec(memory_space=pl.ANY)] * 2,
        out_specs=[pl.BlockSpec(memory_space=pltpu.VMEM)] * 2,
        scratch_shapes=[pltpu.SemaphoreType.DMA((4,))],
    )(previous, current)
    swap = [(i, (i + 1 if i % 2 else i - 1) % size) for i in range(size)]
    return lax.ppermute(far, SITE, swap), lax.ppermute(near, "core", [(0, 1), (1, 0)])


def window_kernel(previous_ref, current_ref, far_ref, near_ref, weight_ref, out_ref, even, odd):
    rows = current_ref.shape[0]
    depth = STEPS
    core = lax.axis_index("core")

    def place(before_ref, after_ref):
        even[pl.ds(0, depth)] = before_ref[pl.ds(depth - 1, depth)]
        even[pl.ds(depth + rows, depth)] = after_ref[pl.ds(depth - 1, depth)]
        odd[pl.ds(1, depth - 1)] = before_ref[pl.ds(0, depth - 1)]
        odd[pl.ds(depth + rows, depth - 1)] = after_ref[pl.ds(0, depth - 1)]

    pl.when(core == 0)(lambda: place(far_ref, near_ref))
    pl.when(core == 1)(lambda: place(near_ref, far_ref))
    even[pl.ds(depth, rows)] = current_ref[...]
    odd[pl.ds(depth, rows)] = previous_ref[...]
    for turn in range(STEPS):
        current, previous = (even, odd) if turn % 2 == 0 else (odd, even)
        last = turn == STEPS - 1

        for row in range(turn + 1, rows + 2 * depth - 1 - turn):
            here = current[row]
            neighbours = current[row + 1] + current[row - 1] + pltpu.roll(here, 1, 0) + pltpu.roll(here, here.shape[0] - 1, 0)
            value = weight_ref[turn, :, row : row + 1] * (ENERGY * here - neighbours - previous[row])
            if last:
                out_ref[row - depth] = value
            else:
                previous[row] = value


def window(previous, current, occupancy):
    rows, side, width = current.shape
    far, near = halos(previous, current)
    start = lax.axis_index(SITE) * rows
    around = jnp.concatenate([occupancy[:, side - STEPS :], occupancy, occupancy[:, :STEPS]], axis=1)
    weights = lax.dynamic_slice_in_dim(around, start, rows + 2 * STEPS, 1).astype(jnp.float32).transpose(0, 2, 1)
    slab = pltpu.VMEM((rows + 2 * STEPS, side, width), jnp.float32)
    return pl.pallas_call(
        window_kernel,
        out_shape=jax.ShapeDtypeStruct(current.shape, jnp.float32),
        in_specs=[pl.BlockSpec(memory_space=pltpu.VMEM)] * 5,
        out_specs=pl.BlockSpec(memory_space=pltpu.VMEM),
        scratch_shapes=[slab, slab],
        compiler_params=pltpu.CompilerParams(vmem_limit_bytes=32 * 1024 * 1024),
        cost_estimate=pl.CostEstimate(flops=12_000_000, bytes_accessed=6_000_000, transcendentals=0),
    )(previous, current, far, near, weights)


def core_sum(value):
    core, half = lax.axis_index("core"), value.shape[0] // 2
    give = lax.dynamic_slice_in_dim(value, (1 - core) * half, half, 0)
    keep = lax.dynamic_slice_in_dim(value, core * half, half, 0)
    return keep + lax.ppermute(give, "core", [(0, 1), (1, 0)])


def product(left, right):
    return jnp.dot(left, right, precision=lax.Precision.HIGHEST, preferred_element_type=jnp.float32)


def product_t(left, right):
    dims = (((0,), (0,)), ((), ()))
    return lax.dot_general(left, right, dims, precision=lax.Precision.HIGHEST, preferred_element_type=jnp.float32)


def fetch_panels(flat, panels):
    received = exchange(flat, COL)
    mine = jnp.concatenate([lax.dynamic_index_in_dim(received, panel, 0, False) for panel in panels], axis=0)
    both = gather(gather(mine, "y"), "x")
    return both.reshape(-1, len(panels), received.shape[1], PANEL)


def split3(x):
    high = x.astype(jnp.bfloat16).astype(jnp.float32)
    rest = x - high
    mid = rest.astype(jnp.bfloat16).astype(jnp.float32)
    return high, mid, rest - mid


def outer(left, right):
    a, b, c = split3(left)
    d, e, f = split3(right)
    lhs = jnp.concatenate([a, a, b, a, c, b], axis=0).astype(jnp.bfloat16)
    rhs = jnp.concatenate([d, e, d, f, d, e], axis=0).astype(jnp.bfloat16)
    return lax.dot_general(lhs, rhs, (((0,), (0,)), ((), ())), preferred_element_type=jnp.float32)


def columns_of(rows, lane, first):
    out = []
    for m in range(BLOCK):
        column = jnp.sum(jnp.where(lane == first + m, rows, 0.0), axis=1, keepdims=True)
        out.append(jnp.broadcast_to(column, (BLOCK, 128)))
    return out


def invert_block(columns):
    entry = {}
    for m in range(BLOCK):
        for i in range(m, BLOCK):
            entry[i, m] = jnp.broadcast_to(columns[m][i : i + 1], (BLOCK, 128))
    inv = {}
    for k in range(BLOCK):
        root = lax.rsqrt(entry[k, k])
        for i in range(k + 1, BLOCK):
            entry[i, k] = entry[i, k] * root
        for m in range(k + 1, BLOCK):
            for i in range(m, BLOCK):
                entry[i, m] = entry[i, m] - entry[i, k] * entry[m, k]
        for c in range(k):
            acc = entry[k, c] * inv[c, c]
            for m in range(c + 1, k):
                acc = acc + entry[k, m] * inv[m, c]
            inv[k, c] = -root * acc
        inv[k, k] = root
    return inv


def combine(columns, rows):
    n = rows.shape[1]
    out = None
    for k in range(BLOCK):
        wide = jnp.concatenate([columns[k]] * (n // 128), axis=1)
        term = wide * jnp.broadcast_to(rows[k : k + 1], (BLOCK, n))
        out = term if out is None else out + term
    return out


def eliminate(out_ref, growth_ref):
    n = out_ref.shape[0]
    lane = lax.broadcasted_iota(jnp.int32, (BLOCK, n), 1)
    sub = lax.broadcasted_iota(jnp.int32, (BLOCK, n), 0)
    sub1 = lax.broadcasted_iota(jnp.int32, (BLOCK, 128), 0)
    lane_all = lax.broadcasted_iota(jnp.int32, (n, n), 1)
    width = GROUP * BLOCK

    def step(j, _):
        first = pl.multiple_of(j * width, width)
        end = first + width
        panels = [out_ref[pl.ds(first + g * BLOCK, BLOCK), :] for g in range(GROUP)]
        done, ahead, rest = [], [], []
        for g in range(GROUP):
            r = first + g * BLOCK
            panel = panels[g]
            inside = jnp.logical_and(lane >= r, lane < r + BLOCK)
            inv = invert_block(columns_of(panel, lane, r))
            below = [columns_of(panels[h], lane, r) for h in range(g + 1, GROUP)]
            panel = jnp.where(inside, jnp.where(lane - r == sub, 1.0, 0.0), panel)
            factor_columns = []
            for k in range(BLOCK):
                column = jnp.zeros((BLOCK, 128), jnp.float32)
                for i in range(k, BLOCK):
                    column = jnp.where(sub1 == i, inv[i, k], column)
                factor_columns.append(column)
            new = combine(factor_columns, panel)
            for h in range(g + 1, GROUP):
                source = below[h - g - 1]
                weights = []
                for k in range(BLOCK):
                    acc = inv[k, 0] * source[0]
                    for m in range(1, k + 1):
                        acc = acc + inv[k, m] * source[m]
                    weights.append(acc)
                panels[h] = jnp.where(inside, 0.0, panels[h]) - combine(weights, new)
            done.append(jnp.where(lane < r + BLOCK, new, 0.0))
            ahead.append(jnp.where(lane >= end, new, 0.0))
            rest.append(jnp.where(jnp.logical_and(lane >= r + BLOCK, lane < end), 0.0, new))
        inside = jnp.logical_and(lane_all >= first, lane_all < end)
        update = outer(jnp.concatenate(ahead, axis=0), jnp.concatenate(rest, axis=0))
        out_ref[...] = jnp.where(inside, 0.0, out_ref[...]) - update
        for g in range(GROUP):
            out_ref[pl.ds(first + g * BLOCK, BLOCK), :] = done[g]
        return 0

    lax.fori_loop(0, n // width, step, 0)
    row = lax.broadcasted_iota(jnp.int32, (n, n), 0)
    growth_ref[...] = -jnp.log(jnp.sum(jnp.where(row == lane_all, out_ref[...], 0.0), axis=0, keepdims=True))


def gram_kernel(both_ref, out_ref):
    half = PANEL // 2
    a, b = [both_ref[:, n].reshape(-1, PANEL) for n in range(2)]
    out_ref[pl.ds(0, half), :] = product_t(a[:, :half], a)
    out_ref[pl.ds(half, half), :] = product_t(b[:, :half], b)
    out_ref[pl.ds(PANEL, half), pl.ds(0, half)] = product_t(a[:, half:], a[:, half:])
    out_ref[pl.ds(PANEL, half), pl.ds(half, half)] = product_t(b[:, half:], b[:, half:])
    out_ref[pl.ds(PANEL + half, PANEL), :] = product_t(a, b)


def first_kernel(gram_ref, out_ref, growth_ref):
    half = PANEL // 2
    out_ref[pl.ds(0, half), :] = gram_ref[pl.ds(0, half), :]
    out_ref[pl.ds(half, half), pl.ds(0, half)] = jnp.zeros((half, half), jnp.float32)
    out_ref[pl.ds(half, half), pl.ds(half, half)] = gram_ref[pl.ds(PANEL, half), pl.ds(0, half)]
    eliminate(out_ref, growth_ref)


def second_kernel(gram_ref, inverse_ref, out_ref, growth_ref, cross_ref):
    half = PANEL // 2
    cross = product(inverse_ref[...], gram_ref[pl.ds(PANEL + half, PANEL), :])
    cross_ref[...] = cross
    inner = product_t(cross, cross)
    out_ref[pl.ds(0, half), :] = gram_ref[pl.ds(half, half), :] - inner[:half]
    out_ref[pl.ds(half, half), pl.ds(0, half)] = jnp.zeros((half, half), jnp.float32)
    out_ref[pl.ds(half, half), pl.ds(half, half)] = gram_ref[pl.ds(PANEL, half), pl.ds(half, half)] - inner[half:, half:]
    eliminate(out_ref, growth_ref)


def on_chip(kernel, flops, *shapes):
    vmem = pl.BlockSpec(memory_space=pltpu.VMEM)
    return lambda *args: pl.pallas_call(
        kernel,
        out_shape=[jax.ShapeDtypeStruct(shape, jnp.float32) for shape in shapes],
        in_specs=[vmem] * len(args),
        out_specs=[vmem] * len(shapes),
        compiler_params=pltpu.CompilerParams(vmem_limit_bytes=32 * 1024 * 1024),
        cost_estimate=pl.CostEstimate(flops=flops, bytes_accessed=524288, transcendentals=PANEL),
    )(*args)


def on_device(state_prev, state_cur, occupancy, panel_order):
    rows, side, width = state_cur.shape
    current = window(state_prev, state_cur, occupancy)
    flat = current.reshape(rows * side, width)
    first, second = panel_order[0], panel_order[1]
    both = fetch_panels(flat, (first, second))
    (gram,) = on_chip(gram_kernel, 4_000_000_000, (PANEL * 5 // 2, PANEL))(both)
    a, b = [both[:, n].reshape(-1, PANEL) for n in range(2)]
    gram = exchange(gram, "core").sum(axis=0)
    a_late, b_late, gram = lax.optimization_barrier((a, b, gram))
    inner = jnp.concatenate([product_t(a_late, flat), product_t(b_late, flat)], axis=0)
    gram = gather(exchange(gram, "z").sum(axis=0), "z")
    inner, gram = lax.optimization_barrier((core_sum(inner), gram))
    gram = lax.all_gather(gram, "core", axis=0, tiled=True)
    inner = exchange(inner, "z").sum(axis=0)
    square, row = (PANEL, PANEL), (1, PANEL)
    inverse_1, growth_1 = on_chip(first_kernel, 1000, square, row)(gram)
    inner, inverse_1 = lax.optimization_barrier((inner, inverse_1))
    inverse_2, growth_2, cross = on_chip(second_kernel, 1000, square, row, square)(gram, inverse_1)
    inner, inverse_2 = lax.optimization_barrier((gather(inner, "z"), inverse_2))
    inner = lax.all_gather(inner, "core", axis=0, tiled=True)
    ax, bx = inner[:PANEL], inner[PANEL:]
    inner_1 = product(inverse_1, ax)
    inner_2 = product(inverse_2, bx - product_t(cross, inner_1))

    col = lax.axis_index(COL)
    is_first, is_second = col == first, col == second
    eye = jnp.eye(PANEL, dtype=jnp.float32) * (-float(side))
    zero = jnp.zeros_like(eye)
    inner_1 = jnp.where(is_first, eye, jnp.where(is_second, zero, inner_1 * RESCALE))
    inner_2 = jnp.where(is_first, zero, jnp.where(is_second, eye, inner_2 * RESCALE))
    weight_b = product_t(inverse_2, inner_2)
    weight_a = product_t(inverse_1, inner_1 - product(cross, weight_b))
    scale = jnp.where(jnp.logical_or(is_first, is_second), 0.0, RESCALE)
    both = jnp.concatenate([a, b], axis=1)
    weight = jnp.concatenate([weight_a, weight_b], axis=0)
    result = flat * scale - product(both, weight)
    return (result.reshape(rows, side, width), jnp.concatenate([growth_1, growth_2], axis=0))


def solution(mesh):
    mesh = jax.sharding.Mesh(mesh.devices.reshape(8, 2, 4, 8), SITE + COL)
    return jax.shard_map(
        on_device,
        mesh=mesh,
        in_specs=(P(SITE, None, COL), P(SITE, None, COL), P(), P()),
        out_specs=(P(SITE, None, COL), P()),
        check_vma=False,
    )
```

```python
import functools

import jax
import jax.numpy as jnp
from jax import lax
from jax.experimental import pallas as pl
from jax.experimental.pallas import tpu as pltpu
from jax.sharding import PartitionSpec as P

STEPS = 4
PANEL = 256
ENERGY = 0.5
RESCALE = 0.015625
BLOCK = 8
GROUP = 4

SITE = ("z", "core")
COL = ("x", "y")


def exchange(value, axis):
    size = lax.axis_size(axis)
    out = lax.all_to_all(value, axis, 0, 0, tiled=True)
    return out.reshape((size, value.shape[0] // size) + value.shape[1:])


def gather(value, axis):
    size = lax.axis_size(axis)
    copies = jnp.broadcast_to(value[None], (size,) + value.shape)
    return lax.all_to_all(copies.reshape((-1,) + value.shape[1:]), axis, 0, 0, tiled=True)


def edge_kernel(far, previous_ref, current_ref, old_ref, new_ref, sems):
    rows, depth = current_ref.shape[0], STEPS
    core = lax.axis_index("core")
    side = core if far else 1 - core
    old = previous_ref.at[pl.ds(side * (rows - depth + 1), depth - 1)]
    new = current_ref.at[pl.ds(side * (rows - depth), depth)]
    copies = [pltpu.make_async_copy(new, new_ref, sems.at[0]), pltpu.make_async_copy(old, old_ref, sems.at[1])]
    for copy in copies:
        copy.start()
    for copy in copies:
        copy.wait()


def halos(previous, current):
    size = lax.axis_size(SITE)
    out = []
    for far in (True, False):
        old, new = pl.pallas_call(
            functools.partial(edge_kernel, far),
            out_shape=[jax.ShapeDtypeStruct((n,) + current.shape[1:], jnp.float32) for n in (STEPS - 1, STEPS)],
            in_specs=[pl.BlockSpec(memory_space=pl.ANY)] * 2,
            out_specs=[pl.BlockSpec(memory_space=pltpu.VMEM)] * 2,
            scratch_shapes=[pltpu.SemaphoreType.DMA((2,))],
        )(previous, current)
        swap = [(i, (i + 1 if i % 2 == far else i - 1) % size) for i in range(size)]
        out += [lax.ppermute(old, SITE, swap), lax.ppermute(new, SITE, swap)]
    return out


def window_kernel(previous_ref, current_ref, far_old, far_new, near_old, near_new, weight_ref, out_ref, even, odd):
    rows = current_ref.shape[0]
    depth = STEPS
    core = lax.axis_index("core")

    def place(before_old, before_new, after_old, after_new):
        even[pl.ds(0, depth)] = before_new[...]
        even[pl.ds(depth + rows, depth)] = after_new[...]
        odd[pl.ds(1, depth - 1)] = before_old[...]
        odd[pl.ds(depth + rows, depth - 1)] = after_old[...]

    pl.when(core == 0)(lambda: place(far_old, far_new, near_old, near_new))
    pl.when(core == 1)(lambda: place(near_old, near_new, far_old, far_new))
    even[pl.ds(depth, rows)] = current_ref[...]
    odd[pl.ds(depth, rows)] = previous_ref[...]
    for turn in range(STEPS):
        current, previous = (even, odd) if turn % 2 == 0 else (odd, even)
        last = turn == STEPS - 1

        for row in range(turn + 1, rows + 2 * depth - 1 - turn):
            here = current[row]
            neighbours = current[row + 1] + current[row - 1] + pltpu.roll(here, 1, 0) + pltpu.roll(here, here.shape[0] - 1, 0)
            value = weight_ref[turn, :, row : row + 1] * (ENERGY * here - neighbours - previous[row])
            if last:
                out_ref[row - depth] = value
            else:
                previous[row] = value


def window(previous, current, occupancy):
    rows, side, width = current.shape
    edges = halos(previous, current)
    start = lax.axis_index(SITE) * rows
    around = jnp.concatenate([occupancy[:, side - STEPS :], occupancy, occupancy[:, :STEPS]], axis=1)
    weights = lax.dynamic_slice_in_dim(around, start, rows + 2 * STEPS, 1).astype(jnp.float32).transpose(0, 2, 1)
    slab = pltpu.VMEM((rows + 2 * STEPS, side, width), jnp.float32)
    return pl.pallas_call(
        window_kernel,
        out_shape=jax.ShapeDtypeStruct(current.shape, jnp.float32),
        in_specs=[pl.BlockSpec(memory_space=pltpu.VMEM)] * 7,
        out_specs=pl.BlockSpec(memory_space=pltpu.VMEM),
        scratch_shapes=[slab, slab],
        compiler_params=pltpu.CompilerParams(vmem_limit_bytes=32 * 1024 * 1024),
        cost_estimate=pl.CostEstimate(flops=12_000_000, bytes_accessed=6_000_000, transcendentals=0),
    )(previous, current, *edges, weights)


def core_sum(value):
    core, half = lax.axis_index("core"), value.shape[0] // 2
    give = lax.dynamic_slice_in_dim(value, (1 - core) * half, half, 0)
    keep = lax.dynamic_slice_in_dim(value, core * half, half, 0)
    return keep + lax.ppermute(give, "core", [(0, 1), (1, 0)])


def product(left, right):
    return jnp.dot(left, right, precision=lax.Precision.HIGHEST, preferred_element_type=jnp.float32)


def product_t(left, right):
    dims = (((0,), (0,)), ((), ()))
    return lax.dot_general(left, right, dims, precision=lax.Precision.HIGHEST, preferred_element_type=jnp.float32)


def fetch_panels(flat, panels):
    received = exchange(flat, COL)
    mine = jnp.concatenate([lax.dynamic_index_in_dim(received, panel, 0, False) for panel in panels], axis=0)
    both = gather(gather(mine, "y"), "x")
    return both.reshape(-1, len(panels), received.shape[1], PANEL)


def split3(x):
    high = x.astype(jnp.bfloat16).astype(jnp.float32)
    rest = x - high
    mid = rest.astype(jnp.bfloat16).astype(jnp.float32)
    return high, mid, rest - mid


def outer(left, right):
    a, b, c = split3(left)
    d, e, f = split3(right)
    lhs = jnp.concatenate([a, a, b, a, c, b], axis=0).astype(jnp.bfloat16)
    rhs = jnp.concatenate([d, e, d, f, d, e], axis=0).astype(jnp.bfloat16)
    return lax.dot_general(lhs, rhs, (((0,), (0,)), ((), ())), preferred_element_type=jnp.float32)


def columns_of(rows, lane, first):
    out = []
    for m in range(BLOCK):
        column = jnp.sum(jnp.where(lane == first + m, rows, 0.0), axis=1, keepdims=True)
        out.append(jnp.broadcast_to(column, (BLOCK, 128)))
    return out


def invert_block(columns):
    entry = {}
    for m in range(BLOCK):
        for i in range(m, BLOCK):
            entry[i, m] = jnp.broadcast_to(columns[m][i : i + 1], (BLOCK, 128))
    inv = {}
    for k in range(BLOCK):
        root = lax.rsqrt(entry[k, k])
        for i in range(k + 1, BLOCK):
            entry[i, k] = entry[i, k] * root
        for m in range(k + 1, BLOCK):
            for i in range(m, BLOCK):
                entry[i, m] = entry[i, m] - entry[i, k] * entry[m, k]
        for c in range(k):
            acc = entry[k, c] * inv[c, c]
            for m in range(c + 1, k):
                acc = acc + entry[k, m] * inv[m, c]
            inv[k, c] = -root * acc
        inv[k, k] = root
    return inv


def combine(columns, rows):
    n = rows.shape[1]
    out = None
    for k in range(BLOCK):
        wide = jnp.concatenate([columns[k]] * (n // 128), axis=1)
        term = wide * jnp.broadcast_to(rows[k : k + 1], (BLOCK, n))
        out = term if out is None else out + term
    return out


def eliminate(out_ref, growth_ref):
    n = out_ref.shape[0]
    lane = lax.broadcasted_iota(jnp.int32, (BLOCK, n), 1)
    sub = lax.broadcasted_iota(jnp.int32, (BLOCK, n), 0)
    sub1 = lax.broadcasted_iota(jnp.int32, (BLOCK, 128), 0)
    lane_all = lax.broadcasted_iota(jnp.int32, (n, n), 1)
    width = GROUP * BLOCK

    def step(j, _):
        first = pl.multiple_of(j * width, width)
        end = first + width
        panels = [out_ref[pl.ds(first + g * BLOCK, BLOCK), :] for g in range(GROUP)]
        done, ahead, rest = [], [], []
        for g in range(GROUP):
            r = first + g * BLOCK
            panel = panels[g]
            inside = jnp.logical_and(lane >= r, lane < r + BLOCK)
            inv = invert_block(columns_of(panel, lane, r))
            below = [columns_of(panels[h], lane, r) for h in range(g + 1, GROUP)]
            panel = jnp.where(inside, jnp.where(lane - r == sub, 1.0, 0.0), panel)
            factor_columns = []
            for k in range(BLOCK):
                column = jnp.zeros((BLOCK, 128), jnp.float32)
                for i in range(k, BLOCK):
                    column = jnp.where(sub1 == i, inv[i, k], column)
                factor_columns.append(column)
            new = combine(factor_columns, panel)
            for h in range(g + 1, GROUP):
                source = below[h - g - 1]
                weights = []
                for k in range(BLOCK):
                    acc = inv[k, 0] * source[0]
                    for m in range(1, k + 1):
                        acc = acc + inv[k, m] * source[m]
                    weights.append(acc)
                panels[h] = jnp.where(inside, 0.0, panels[h]) - combine(weights, new)
            done.append(jnp.where(lane < r + BLOCK, new, 0.0))
            ahead.append(jnp.where(lane >= end, new, 0.0))
            rest.append(jnp.where(jnp.logical_and(lane >= r + BLOCK, lane < end), 0.0, new))
        inside = jnp.logical_and(lane_all >= first, lane_all < end)
        update = outer(jnp.concatenate(ahead, axis=0), jnp.concatenate(rest, axis=0))
        out_ref[...] = jnp.where(inside, 0.0, out_ref[...]) - update
        for g in range(GROUP):
            out_ref[pl.ds(first + g * BLOCK, BLOCK), :] = done[g]
        return 0

    lax.fori_loop(0, n // width, step, 0)
    row = lax.broadcasted_iota(jnp.int32, (n, n), 0)
    growth_ref[...] = -jnp.log(jnp.sum(jnp.where(row == lane_all, out_ref[...], 0.0), axis=0, keepdims=True))


def gram_kernel(both_ref, out_ref):
    half = PANEL // 2
    a, b = [both_ref[:, n].reshape(-1, PANEL) for n in range(2)]
    out_ref[pl.ds(0, half), :] = product_t(a[:, :half], a)
    out_ref[pl.ds(half, half), :] = product_t(b[:, :half], b)
    out_ref[pl.ds(PANEL, half), pl.ds(0, half)] = product_t(a[:, half:], a[:, half:])
    out_ref[pl.ds(PANEL, half), pl.ds(half, half)] = product_t(b[:, half:], b[:, half:])
    out_ref[pl.ds(PANEL + half, PANEL), :] = product_t(a, b)


def first_kernel(gram_ref, out_ref, growth_ref):
    half = PANEL // 2
    out_ref[pl.ds(0, half), :] = gram_ref[pl.ds(0, half), :]
    out_ref[pl.ds(half, half), pl.ds(0, half)] = jnp.zeros((half, half), jnp.float32)
    out_ref[pl.ds(half, half), pl.ds(half, half)] = gram_ref[pl.ds(PANEL, half), pl.ds(0, half)]
    eliminate(out_ref, growth_ref)


def second_kernel(gram_ref, inverse_ref, out_ref, growth_ref, cross_ref):
    half = PANEL // 2
    cross = product(inverse_ref[...], gram_ref[pl.ds(PANEL + half, PANEL), :])
    cross_ref[...] = cross
    inner = product_t(cross, cross)
    out_ref[pl.ds(0, half), :] = gram_ref[pl.ds(half, half), :] - inner[:half]
    out_ref[pl.ds(half, half), pl.ds(0, half)] = jnp.zeros((half, half), jnp.float32)
    out_ref[pl.ds(half, half), pl.ds(half, half)] = gram_ref[pl.ds(PANEL, half), pl.ds(half, half)] - inner[half:, half:]
    eliminate(out_ref, growth_ref)


def on_chip(kernel, flops, *shapes):
    vmem = pl.BlockSpec(memory_space=pltpu.VMEM)
    return lambda *args: pl.pallas_call(
        kernel,
        out_shape=[jax.ShapeDtypeStruct(shape, jnp.float32) for shape in shapes],
        in_specs=[vmem] * len(args),
        out_specs=[vmem] * len(shapes),
        compiler_params=pltpu.CompilerParams(vmem_limit_bytes=32 * 1024 * 1024),
        cost_estimate=pl.CostEstimate(flops=flops, bytes_accessed=524288, transcendentals=PANEL),
    )(*args)


def on_device(state_prev, state_cur, occupancy, panel_order):
    rows, side, width = state_cur.shape
    current = window(state_prev, state_cur, occupancy)
    flat = current.reshape(rows * side, width)
    first, second = panel_order[0], panel_order[1]
    both = fetch_panels(flat, (first, second))
    (gram,) = on_chip(gram_kernel, 4_000_000_000, (PANEL * 5 // 2, PANEL))(both)
    a, b = [both[:, n].reshape(-1, PANEL) for n in range(2)]
    gram = exchange(gram, "core").sum(axis=0)
    a_late, b_late, gram = lax.optimization_barrier((a, b, gram))
    inner = jnp.concatenate([product_t(a_late, flat), product_t(b_late, flat)], axis=0)
    gram = gather(exchange(gram, "z").sum(axis=0), "z")
    inner, gram = lax.optimization_barrier((core_sum(inner), gram))
    gram = lax.all_gather(gram, "core", axis=0, tiled=True)
    inner = exchange(inner, "z").sum(axis=0)
    square, row = (PANEL, PANEL), (1, PANEL)
    inverse_1, growth_1 = on_chip(first_kernel, 1000, square, row)(gram)
    inner, inverse_1 = lax.optimization_barrier((inner, inverse_1))
    inverse_2, growth_2, cross = on_chip(second_kernel, 1000, square, row, square)(gram, inverse_1)
    inner, inverse_2 = lax.optimization_barrier((gather(inner, "z"), inverse_2))
    inner = lax.all_gather(inner, "core", axis=0, tiled=True)
    ax, bx = inner[:PANEL], inner[PANEL:]
    inner_1 = product(inverse_1, ax)
    inner_2 = product(inverse_2, bx - product_t(cross, inner_1))

    col = lax.axis_index(COL)
    is_first, is_second = col == first, col == second
    eye = jnp.eye(PANEL, dtype=jnp.float32) * (-float(side))
    zero = jnp.zeros_like(eye)
    inner_1 = jnp.where(is_first, eye, jnp.where(is_second, zero, inner_1 * RESCALE))
    inner_2 = jnp.where(is_first, zero, jnp.where(is_second, eye, inner_2 * RESCALE))
    weight_b = product_t(inverse_2, inner_2)
    weight_a = product_t(inverse_1, inner_1 - product(cross, weight_b))
    scale = jnp.where(jnp.logical_or(is_first, is_second), 0.0, RESCALE)
    both = jnp.concatenate([a, b], axis=1)
    weight = jnp.concatenate([weight_a, weight_b], axis=0)
    result = flat * scale - product(both, weight)
    return (result.reshape(rows, side, width), jnp.concatenate([growth_1, growth_2], axis=0))


def solution(mesh):
    mesh = jax.sharding.Mesh(mesh.devices.reshape(8, 2, 4, 8), SITE + COL)
    return jax.shard_map(
        on_device,
        mesh=mesh,
        in_specs=(P(SITE, None, COL), P(SITE, None, COL), P(), P()),
        out_specs=(P(SITE, None, COL), P()),
        check_vma=False,
    )
```

```python
import jax
import jax.numpy as jnp
from jax import lax
from jax.experimental import pallas as pl
from jax.experimental.pallas import tpu as pltpu
from jax.sharding import PartitionSpec as P

STEPS = 4
PANEL = 256
ENERGY = 0.5
RESCALE = 0.015625
BLOCK = 8
GROUP = 4

SITE = ("z", "core")
COL = ("x", "y")


def exchange(value, axis):
    size = lax.axis_size(axis)
    out = lax.all_to_all(value, axis, 0, 0, tiled=True)
    return out.reshape((size, value.shape[0] // size) + value.shape[1:])


def gather(value, axis):
    size = lax.axis_size(axis)
    copies = jnp.broadcast_to(value[None], (size,) + value.shape)
    return lax.all_to_all(copies.reshape((-1,) + value.shape[1:]), axis, 0, 0, tiled=True)


def edges_kernel(previous_ref, current_ref, far_old, far_new, near_ref, sems):
    rows, depth = current_ref.shape[0], STEPS
    core = lax.axis_index("core")

    def edge(ref, count, side):
        return ref.at[pl.ds(side * (rows - count), count)]

    near_old, near_new = near_ref.at[pl.ds(0, depth - 1)], near_ref.at[pl.ds(depth - 1, depth)]
    copies = [
        pltpu.make_async_copy(edge(current_ref, depth, core), far_new, sems.at[0]),
        pltpu.make_async_copy(edge(previous_ref, depth - 1, core), far_old, sems.at[1]),
        pltpu.make_async_copy(edge(current_ref, depth, 1 - core), near_new, sems.at[2]),
        pltpu.make_async_copy(edge(previous_ref, depth - 1, 1 - core), near_old, sems.at[3]),
    ]
    for copy in copies:
        copy.start()
    for copy in copies:
        copy.wait()


def halos(previous, current):
    size = lax.axis_size(SITE)
    counts = (STEPS - 1, STEPS, 2 * STEPS - 1)
    far_old, far_new, near = pl.pallas_call(
        edges_kernel,
        out_shape=[jax.ShapeDtypeStruct((n,) + current.shape[1:], jnp.float32) for n in counts],
        in_specs=[pl.BlockSpec(memory_space=pl.ANY)] * 2,
        out_specs=[pl.BlockSpec(memory_space=pltpu.VMEM)] * 3,
        scratch_shapes=[pltpu.SemaphoreType.DMA((4,))],
    )(previous, current)
    swap = [(i, (i + 1 if i % 2 else i - 1) % size) for i in range(size)]
    return [lax.ppermute(near, "core", [(0, 1), (1, 0)]), lax.ppermute(far_old, SITE, swap), lax.ppermute(far_new, SITE, swap)]


def window_kernel(near_ref, far_old, far_new, occupancy_ref, previous_ref, current_ref, out_ref, even, odd):
    rows, side = current_ref.shape[0], current_ref.shape[1]
    depth = STEPS
    core, size = lax.axis_index("core"), lax.axis_size("z") * lax.axis_size("core")
    site = lax.axis_index("z") * lax.axis_size("core") + core
    near_old, near_new = near_ref.at[pl.ds(0, depth - 1)], near_ref.at[pl.ds(depth - 1, depth)]

    def place(before_old, before_new, after_old, after_new):
        even[pl.ds(0, depth)] = before_new[...]
        even[pl.ds(depth + rows, depth)] = after_new[...]
        odd[pl.ds(1, depth - 1)] = before_old[...]
        odd[pl.ds(depth + rows, depth - 1)] = after_old[...]

    pl.when(core == 0)(lambda: place(far_old, far_new, near_old, near_new))
    pl.when(core == 1)(lambda: place(near_old, near_new, far_old, far_new))

    slabs = [lax.rem(site + size - 1, size), site, lax.rem(site + 1, size)]
    unread = jnp.zeros((side - len(slabs) * rows, side), jnp.float32)

    for turn in range(STEPS):
        masks = [occupancy_ref[turn, pl.ds(pl.multiple_of(slab * rows, rows), rows), :].astype(jnp.float32) for slab in slabs]
        weights = jnp.concatenate(masks + [unread], axis=0).T
        current, previous = (even, odd) if turn % 2 == 0 else (odd, even)

        def load(now, row):
            own = depth <= row < depth + rows
            if own and turn == 0:
                return current_ref[row - depth] if now else previous_ref[row - depth]
            if own and turn == 1 and not now:
                return current_ref[row - depth]
            return (current if now else previous)[row]

        for row in range(turn + 1, rows + 2 * depth - 1 - turn):
            here = load(True, row)
            neighbours = load(True, row + 1) + load(True, row - 1) + pltpu.roll(here, 1, 0) + pltpu.roll(here, side - 1, 0)
            column = row + rows - depth
            value = weights[:, column : column + 1] * (ENERGY * here - neighbours - load(False, row))
            if turn == STEPS - 1:
                out_ref[row - depth] = value
            else:
                previous[row] = value


def window(previous, current, occupancy):
    rows, side, width = current.shape
    slab = pltpu.VMEM((rows + 2 * STEPS, side, width), jnp.float32)
    return pl.pallas_call(
        window_kernel,
        out_shape=jax.ShapeDtypeStruct(current.shape, jnp.float32),
        in_specs=[pl.BlockSpec(memory_space=pltpu.VMEM)] * 6,
        out_specs=pl.BlockSpec(memory_space=pltpu.VMEM),
        scratch_shapes=[slab, slab],
        compiler_params=pltpu.CompilerParams(vmem_limit_bytes=32 * 1024 * 1024),
        cost_estimate=pl.CostEstimate(flops=12_000_000, bytes_accessed=6_000_000, transcendentals=0),
    )(*halos(previous, current), occupancy, previous, current)


def core_sum(value):
    core, half = lax.axis_index("core"), value.shape[0] // 2
    give = lax.dynamic_slice_in_dim(value, (1 - core) * half, half, 0)
    keep = lax.dynamic_slice_in_dim(value, core * half, half, 0)
    return keep + lax.ppermute(give, "core", [(0, 1), (1, 0)])


def product(left, right):
    return jnp.dot(left, right, precision=lax.Precision.HIGHEST, preferred_element_type=jnp.float32)


def product_t(left, right):
    dims = (((0,), (0,)), ((), ()))
    return lax.dot_general(left, right, dims, precision=lax.Precision.HIGHEST, preferred_element_type=jnp.float32)


def fetch_panels(flat, panels):
    received = exchange(flat, COL)
    mine = jnp.concatenate([lax.dynamic_index_in_dim(received, panel, 0, False) for panel in panels], axis=0)
    both = gather(gather(mine, "y"), "x")
    return both.reshape(-1, len(panels), received.shape[1], PANEL)


def split3(x):
    high = x.astype(jnp.bfloat16).astype(jnp.float32)
    rest = x - high
    mid = rest.astype(jnp.bfloat16).astype(jnp.float32)
    return high, mid, rest - mid


def outer(left, right):
    a, b, c = split3(left)
    d, e, f = split3(right)
    lhs = jnp.concatenate([a, a, b, a, c, b], axis=0).astype(jnp.bfloat16)
    rhs = jnp.concatenate([d, e, d, f, d, e], axis=0).astype(jnp.bfloat16)
    return lax.dot_general(lhs, rhs, (((0,), (0,)), ((), ())), preferred_element_type=jnp.float32)


def columns_of(rows, lane, first):
    out = []
    for m in range(BLOCK):
        column = jnp.sum(jnp.where(lane == first + m, rows, 0.0), axis=1, keepdims=True)
        out.append(jnp.broadcast_to(column, (BLOCK, 128)))
    return out


def invert_block(columns):
    entry = {}
    for m in range(BLOCK):
        for i in range(m, BLOCK):
            entry[i, m] = jnp.broadcast_to(columns[m][i : i + 1], (BLOCK, 128))
    inv = {}
    for k in range(BLOCK):
        root = lax.rsqrt(entry[k, k])
        for i in range(k + 1, BLOCK):
            entry[i, k] = entry[i, k] * root
        for m in range(k + 1, BLOCK):
            for i in range(m, BLOCK):
                entry[i, m] = entry[i, m] - entry[i, k] * entry[m, k]
        for c in range(k):
            acc = entry[k, c] * inv[c, c]
            for m in range(c + 1, k):
                acc = acc + entry[k, m] * inv[m, c]
            inv[k, c] = -root * acc
        inv[k, k] = root
    return inv


def combine(columns, rows):
    n = rows.shape[1]
    out = None
    for k in range(BLOCK):
        wide = jnp.concatenate([columns[k]] * (n // 128), axis=1)
        term = wide * jnp.broadcast_to(rows[k : k + 1], (BLOCK, n))
        out = term if out is None else out + term
    return out


def eliminate(out_ref, growth_ref):
    n = out_ref.shape[0]
    lane = lax.broadcasted_iota(jnp.int32, (BLOCK, n), 1)
    sub = lax.broadcasted_iota(jnp.int32, (BLOCK, n), 0)
    sub1 = lax.broadcasted_iota(jnp.int32, (BLOCK, 128), 0)
    lane_all = lax.broadcasted_iota(jnp.int32, (n, n), 1)
    width = GROUP * BLOCK

    def step(j, _):
        first = pl.multiple_of(j * width, width)
        end = first + width
        panels = [out_ref[pl.ds(first + g * BLOCK, BLOCK), :] for g in range(GROUP)]
        done, ahead, rest = [], [], []
        for g in range(GROUP):
            r = first + g * BLOCK
            panel = panels[g]
            inside = jnp.logical_and(lane >= r, lane < r + BLOCK)
            inv = invert_block(columns_of(panel, lane, r))
            below = [columns_of(panels[h], lane, r) for h in range(g + 1, GROUP)]
            panel = jnp.where(inside, jnp.where(lane - r == sub, 1.0, 0.0), panel)
            factor_columns = []
            for k in range(BLOCK):
                column = jnp.zeros((BLOCK, 128), jnp.float32)
                for i in range(k, BLOCK):
                    column = jnp.where(sub1 == i, inv[i, k], column)
                factor_columns.append(column)
            new = combine(factor_columns, panel)
            for h in range(g + 1, GROUP):
                source = below[h - g - 1]
                weights = []
                for k in range(BLOCK):
                    acc = inv[k, 0] * source[0]
                    for m in range(1, k + 1):
                        acc = acc + inv[k, m] * source[m]
                    weights.append(acc)
                panels[h] = jnp.where(inside, 0.0, panels[h]) - combine(weights, new)
            done.append(jnp.where(lane < r + BLOCK, new, 0.0))
            ahead.append(jnp.where(lane >= end, new, 0.0))
            rest.append(jnp.where(jnp.logical_and(lane >= r + BLOCK, lane < end), 0.0, new))
        inside = jnp.logical_and(lane_all >= first, lane_all < end)
        update = outer(jnp.concatenate(ahead, axis=0), jnp.concatenate(rest, axis=0))
        out_ref[...] = jnp.where(inside, 0.0, out_ref[...]) - update
        for g in range(GROUP):
            out_ref[pl.ds(first + g * BLOCK, BLOCK), :] = done[g]
        return 0

    lax.fori_loop(0, n // width, step, 0)
    row = lax.broadcasted_iota(jnp.int32, (n, n), 0)
    growth_ref[...] = -jnp.log(jnp.sum(jnp.where(row == lane_all, out_ref[...], 0.0), axis=0, keepdims=True))


def gram_kernel(both_ref, out_ref):
    half = PANEL // 2
    a, b = [both_ref[:, n].reshape(-1, PANEL) for n in range(2)]
    out_ref[pl.ds(0, half), :] = product_t(a[:, :half], a)
    out_ref[pl.ds(half, half), :] = product_t(b[:, :half], b)
    out_ref[pl.ds(PANEL, half), pl.ds(0, half)] = product_t(a[:, half:], a[:, half:])
    out_ref[pl.ds(PANEL, half), pl.ds(half, half)] = product_t(b[:, half:], b[:, half:])
    out_ref[pl.ds(PANEL + half, PANEL), :] = product_t(a, b)


def first_kernel(gram_ref, out_ref, growth_ref):
    half = PANEL // 2
    out_ref[pl.ds(0, half), :] = gram_ref[pl.ds(0, half), :]
    out_ref[pl.ds(half, half), pl.ds(0, half)] = jnp.zeros((half, half), jnp.float32)
    out_ref[pl.ds(half, half), pl.ds(half, half)] = gram_ref[pl.ds(PANEL, half), pl.ds(0, half)]
    eliminate(out_ref, growth_ref)


def second_kernel(gram_ref, inverse_ref, out_ref, growth_ref, cross_ref):
    half = PANEL // 2
    cross = product(inverse_ref[...], gram_ref[pl.ds(PANEL + half, PANEL), :])
    cross_ref[...] = cross
    inner = product_t(cross, cross)
    out_ref[pl.ds(0, half), :] = gram_ref[pl.ds(half, half), :] - inner[:half]
    out_ref[pl.ds(half, half), pl.ds(0, half)] = jnp.zeros((half, half), jnp.float32)
    out_ref[pl.ds(half, half), pl.ds(half, half)] = gram_ref[pl.ds(PANEL, half), pl.ds(half, half)] - inner[half:, half:]
    eliminate(out_ref, growth_ref)


def on_chip(kernel, flops, *shapes):
    vmem = pl.BlockSpec(memory_space=pltpu.VMEM)
    return lambda *args: pl.pallas_call(
        kernel,
        out_shape=[jax.ShapeDtypeStruct(shape, jnp.float32) for shape in shapes],
        in_specs=[vmem] * len(args),
        out_specs=[vmem] * len(shapes),
        compiler_params=pltpu.CompilerParams(vmem_limit_bytes=32 * 1024 * 1024),
        cost_estimate=pl.CostEstimate(flops=flops, bytes_accessed=524288, transcendentals=PANEL),
    )(*args)


def on_device(state_prev, state_cur, occupancy, panel_order):
    rows, side, width = state_cur.shape
    current = window(state_prev, state_cur, occupancy)
    flat = current.reshape(rows * side, width)
    first, second = panel_order[0], panel_order[1]
    both = fetch_panels(flat, (first, second))
    (gram,) = on_chip(gram_kernel, 4_000_000_000, (PANEL * 5 // 2, PANEL))(both)
    a, b = [both[:, n].reshape(-1, PANEL) for n in range(2)]
    gram = exchange(gram, "core").sum(axis=0)
    a_late, b_late, gram = lax.optimization_barrier((a, b, gram))
    inner = jnp.concatenate([product_t(a_late, flat), product_t(b_late, flat)], axis=0)
    gram = gather(exchange(gram, "z").sum(axis=0), "z")
    inner, gram = lax.optimization_barrier((core_sum(inner), gram))
    gram = lax.all_gather(gram, "core", axis=0, tiled=True)
    inner = exchange(inner, "z").sum(axis=0)
    square, row = (PANEL, PANEL), (1, PANEL)
    inverse_1, growth_1 = on_chip(first_kernel, 1000, square, row)(gram)
    inner, inverse_1 = lax.optimization_barrier((inner, inverse_1))
    inverse_2, growth_2, cross = on_chip(second_kernel, 1000, square, row, square)(gram, inverse_1)
    inner, inverse_2 = lax.optimization_barrier((gather(inner, "z"), inverse_2))
    inner = lax.all_gather(inner, "core", axis=0, tiled=True)
    ax, bx = inner[:PANEL], inner[PANEL:]
    inner_1 = product(inverse_1, ax)
    inner_2 = product(inverse_2, bx - product_t(cross, inner_1))

    col = lax.axis_index(COL)
    is_first, is_second = col == first, col == second
    eye = jnp.eye(PANEL, dtype=jnp.float32) * (-float(side))
    zero = jnp.zeros_like(eye)
    inner_1 = jnp.where(is_first, eye, jnp.where(is_second, zero, inner_1 * RESCALE))
    inner_2 = jnp.where(is_first, zero, jnp.where(is_second, eye, inner_2 * RESCALE))
    weight_b = product_t(inverse_2, inner_2)
    weight_a = product_t(inverse_1, inner_1 - product(cross, weight_b))
    scale = jnp.where(jnp.logical_or(is_first, is_second), 0.0, RESCALE)
    both = jnp.concatenate([a, b], axis=1)
    weight = jnp.concatenate([weight_a, weight_b], axis=0)
    result = flat * scale - product(both, weight)
    return (result.reshape(rows, side, width), jnp.concatenate([growth_1, growth_2], axis=0))


def solution(mesh):
    mesh = jax.sharding.Mesh(mesh.devices.reshape(8, 2, 4, 8), SITE + COL)
    return jax.shard_map(
        on_device,
        mesh=mesh,
        in_specs=(P(SITE, None, COL), P(SITE, None, COL), P(), P()),
        out_specs=(P(SITE, None, COL), P()),
        check_vma=False,
    )
```

```python
import functools

import jax
import jax.numpy as jnp
from jax import lax
from jax.experimental import pallas as pl
from jax.experimental.pallas import tpu as pltpu
from jax.sharding import PartitionSpec as P

STEPS = 4
PANEL = 256
ENERGY = 0.5
RESCALE = 0.015625
BLOCK = 8
GROUP = 4

SITE = ("z", "core")
COL = ("x", "y")


def exchange(value, axis):
    size = lax.axis_size(axis)
    out = lax.all_to_all(value, axis, 0, 0, tiled=True)
    return out.reshape((size, value.shape[0] // size) + value.shape[1:])


def gather(value, axis):
    size = lax.axis_size(axis)
    copies = jnp.broadcast_to(value[None], (size,) + value.shape)
    return lax.all_to_all(copies.reshape((-1,) + value.shape[1:]), axis, 0, 0, tiled=True)


def edge_kernel(far, previous_ref, current_ref, out_ref, sems):
    rows, depth = current_ref.shape[0], STEPS
    core = lax.axis_index("core")
    side = core if far else 1 - core
    old = previous_ref.at[pl.ds(side * (rows - depth + 1), depth - 1)]
    new = current_ref.at[pl.ds(side * (rows - depth), depth)]
    copies = [
        pltpu.make_async_copy(old, out_ref.at[pl.ds(0, depth - 1)], sems.at[0]),
        pltpu.make_async_copy(new, out_ref.at[pl.ds(depth - 1, depth)], sems.at[1]),
    ]
    for copy in copies:
        copy.start()
    for copy in copies:
        copy.wait()


def halos(previous, current):
    size = lax.axis_size(SITE)
    out = []
    for far in (True, False):
        edge = pl.pallas_call(
            functools.partial(edge_kernel, far),
            out_shape=jax.ShapeDtypeStruct((2 * STEPS - 1,) + current.shape[1:], jnp.float32),
            in_specs=[pl.BlockSpec(memory_space=pl.ANY)] * 2,
            out_specs=pl.BlockSpec(memory_space=pltpu.VMEM),
            scratch_shapes=[pltpu.SemaphoreType.DMA((2,))],
        )(previous, current)
        swap = [(i, (i + 1 if i % 2 == far else i - 1) % size) for i in range(size)]
        out.append(lax.ppermute(edge, SITE, swap))
    return out


def window_kernel(previous_ref, current_ref, far_ref, near_ref, occupancy_ref, out_ref, even, odd, masks_ref, sem):
    rows, side = current_ref.shape[0], current_ref.shape[1]
    depth = STEPS
    core, size = lax.axis_index("core"), lax.axis_size("z") * lax.axis_size("core")
    site = lax.axis_index("z") * lax.axis_size("core") + core
    fetch = pltpu.make_async_copy(occupancy_ref, masks_ref, sem)
    fetch.start()

    def place(before_ref, after_ref):
        even[pl.ds(0, depth)] = before_ref[pl.ds(depth - 1, depth)]
        even[pl.ds(depth + rows, depth)] = after_ref[pl.ds(depth - 1, depth)]
        odd[pl.ds(1, depth - 1)] = before_ref[pl.ds(0, depth - 1)]
        odd[pl.ds(depth + rows, depth - 1)] = after_ref[pl.ds(0, depth - 1)]

    pl.when(core == 0)(lambda: place(far_ref, near_ref))
    pl.when(core == 1)(lambda: place(near_ref, far_ref))
    fetch.wait()

    slabs = [lax.rem(site + size - 1, size), site, lax.rem(site + 1, size)]
    unread = jnp.zeros((side - len(slabs) * rows, side), jnp.float32)

    for turn in range(STEPS):
        masks = [masks_ref[turn, pl.ds(pl.multiple_of(slab * rows, rows), rows), :].astype(jnp.float32) for slab in slabs]
        weights = jnp.concatenate(masks + [unread], axis=0).T
        current, previous = (even, odd) if turn % 2 == 0 else (odd, even)

        def load(now, row):
            own = depth <= row < depth + rows
            if own and turn == 0:
                return current_ref[row - depth] if now else previous_ref[row - depth]
            if own and turn == 1 and not now:
                return current_ref[row - depth]
            return (current if now else previous)[row]

        for row in range(turn + 1, rows + 2 * depth - 1 - turn):
            here = load(True, row)
            neighbours = load(True, row + 1) + load(True, row - 1) + pltpu.roll(here, 1, 0) + pltpu.roll(here, side - 1, 0)
            column = row + rows - depth
            value = weights[:, column : column + 1] * (ENERGY * here - neighbours - load(False, row))
            if turn == STEPS - 1:
                out_ref[row - depth] = value
            else:
                previous[row] = value


def window(previous, current, occupancy):
    rows, side, width = current.shape
    slab = pltpu.VMEM((rows + 2 * STEPS, side, width), jnp.float32)
    return pl.pallas_call(
        window_kernel,
        out_shape=jax.ShapeDtypeStruct(current.shape, jnp.float32),
        in_specs=[pl.BlockSpec(memory_space=pltpu.VMEM)] * 4 + [pl.BlockSpec(memory_space=pl.ANY)],
        out_specs=pl.BlockSpec(memory_space=pltpu.VMEM),
        scratch_shapes=[slab, slab, pltpu.VMEM(occupancy.shape, jnp.int32), pltpu.SemaphoreType.DMA],
        compiler_params=pltpu.CompilerParams(vmem_limit_bytes=32 * 1024 * 1024),
        cost_estimate=pl.CostEstimate(flops=12_000_000, bytes_accessed=6_000_000, transcendentals=0),
    )(previous, current, *halos(previous, current), occupancy)


def core_sum(value):
    core, half = lax.axis_index("core"), value.shape[0] // 2
    give = lax.dynamic_slice_in_dim(value, (1 - core) * half, half, 0)
    keep = lax.dynamic_slice_in_dim(value, core * half, half, 0)
    return keep + lax.ppermute(give, "core", [(0, 1), (1, 0)])


def product(left, right):
    return jnp.dot(left, right, precision=lax.Precision.HIGHEST, preferred_element_type=jnp.float32)


def product_t(left, right):
    dims = (((0,), (0,)), ((), ()))
    return lax.dot_general(left, right, dims, precision=lax.Precision.HIGHEST, preferred_element_type=jnp.float32)


def fetch_panels(flat, panels):
    received = exchange(flat, COL)
    mine = jnp.concatenate([lax.dynamic_index_in_dim(received, panel, 0, False) for panel in panels], axis=0)
    both = gather(gather(mine, "y"), "x")
    return both.reshape(-1, len(panels), received.shape[1], PANEL)


def split3(x):
    high = x.astype(jnp.bfloat16).astype(jnp.float32)
    rest = x - high
    mid = rest.astype(jnp.bfloat16).astype(jnp.float32)
    return high, mid, rest - mid


def outer(left, right):
    a, b, c = split3(left)
    d, e, f = split3(right)
    lhs = jnp.concatenate([a, a, b, a, c, b], axis=0).astype(jnp.bfloat16)
    rhs = jnp.concatenate([d, e, d, f, d, e], axis=0).astype(jnp.bfloat16)
    return lax.dot_general(lhs, rhs, (((0,), (0,)), ((), ())), preferred_element_type=jnp.float32)


def columns_of(rows, lane, first):
    out = []
    for m in range(BLOCK):
        column = jnp.sum(jnp.where(lane == first + m, rows, 0.0), axis=1, keepdims=True)
        out.append(jnp.broadcast_to(column, (BLOCK, 128)))
    return out


def invert_block(columns):
    entry = {}
    for m in range(BLOCK):
        for i in range(m, BLOCK):
            entry[i, m] = jnp.broadcast_to(columns[m][i : i + 1], (BLOCK, 128))
    inv = {}
    for k in range(BLOCK):
        root = lax.rsqrt(entry[k, k])
        for i in range(k + 1, BLOCK):
            entry[i, k] = entry[i, k] * root
        for m in range(k + 1, BLOCK):
            for i in range(m, BLOCK):
                entry[i, m] = entry[i, m] - entry[i, k] * entry[m, k]
        for c in range(k):
            acc = entry[k, c] * inv[c, c]
            for m in range(c + 1, k):
                acc = acc + entry[k, m] * inv[m, c]
            inv[k, c] = -root * acc
        inv[k, k] = root
    return inv


def combine(columns, rows):
    n = rows.shape[1]
    out = None
    for k in range(BLOCK):
        wide = jnp.concatenate([columns[k]] * (n // 128), axis=1)
        term = wide * jnp.broadcast_to(rows[k : k + 1], (BLOCK, n))
        out = term if out is None else out + term
    return out


def eliminate(out_ref, growth_ref):
    n = out_ref.shape[0]
    lane = lax.broadcasted_iota(jnp.int32, (BLOCK, n), 1)
    sub = lax.broadcasted_iota(jnp.int32, (BLOCK, n), 0)
    sub1 = lax.broadcasted_iota(jnp.int32, (BLOCK, 128), 0)
    lane_all = lax.broadcasted_iota(jnp.int32, (n, n), 1)
    width = GROUP * BLOCK

    def step(j, _):
        first = pl.multiple_of(j * width, width)
        end = first + width
        panels = [out_ref[pl.ds(first + g * BLOCK, BLOCK), :] for g in range(GROUP)]
        done, ahead, rest = [], [], []
        for g in range(GROUP):
            r = first + g * BLOCK
            panel = panels[g]
            inside = jnp.logical_and(lane >= r, lane < r + BLOCK)
            inv = invert_block(columns_of(panel, lane, r))
            below = [columns_of(panels[h], lane, r) for h in range(g + 1, GROUP)]
            panel = jnp.where(inside, jnp.where(lane - r == sub, 1.0, 0.0), panel)
            factor_columns = []
            for k in range(BLOCK):
                column = jnp.zeros((BLOCK, 128), jnp.float32)
                for i in range(k, BLOCK):
                    column = jnp.where(sub1 == i, inv[i, k], column)
                factor_columns.append(column)
            new = combine(factor_columns, panel)
            for h in range(g + 1, GROUP):
                source = below[h - g - 1]
                weights = []
                for k in range(BLOCK):
                    acc = inv[k, 0] * source[0]
                    for m in range(1, k + 1):
                        acc = acc + inv[k, m] * source[m]
                    weights.append(acc)
                panels[h] = jnp.where(inside, 0.0, panels[h]) - combine(weights, new)
            done.append(jnp.where(lane < r + BLOCK, new, 0.0))
            ahead.append(jnp.where(lane >= end, new, 0.0))
            rest.append(jnp.where(jnp.logical_and(lane >= r + BLOCK, lane < end), 0.0, new))
        inside = jnp.logical_and(lane_all >= first, lane_all < end)
        update = outer(jnp.concatenate(ahead, axis=0), jnp.concatenate(rest, axis=0))
        out_ref[...] = jnp.where(inside, 0.0, out_ref[...]) - update
        for g in range(GROUP):
            out_ref[pl.ds(first + g * BLOCK, BLOCK), :] = done[g]
        return 0

    lax.fori_loop(0, n // width, step, 0)
    row = lax.broadcasted_iota(jnp.int32, (n, n), 0)
    growth_ref[...] = -jnp.log(jnp.sum(jnp.where(row == lane_all, out_ref[...], 0.0), axis=0, keepdims=True))


def gram_kernel(both_ref, out_ref):
    half = PANEL // 2
    a, b = [both_ref[:, n].reshape(-1, PANEL) for n in range(2)]
    out_ref[pl.ds(0, half), :] = product_t(a[:, :half], a)
    out_ref[pl.ds(half, half), :] = product_t(b[:, :half], b)
    out_ref[pl.ds(PANEL, half), pl.ds(0, half)] = product_t(a[:, half:], a[:, half:])
    out_ref[pl.ds(PANEL, half), pl.ds(half, half)] = product_t(b[:, half:], b[:, half:])
    out_ref[pl.ds(PANEL + half, PANEL), :] = product_t(a, b)


def first_kernel(gram_ref, out_ref, growth_ref):
    half = PANEL // 2
    out_ref[pl.ds(0, half), :] = gram_ref[pl.ds(0, half), :]
    out_ref[pl.ds(half, half), pl.ds(0, half)] = jnp.zeros((half, half), jnp.float32)
    out_ref[pl.ds(half, half), pl.ds(half, half)] = gram_ref[pl.ds(PANEL, half), pl.ds(0, half)]
    eliminate(out_ref, growth_ref)


def second_kernel(gram_ref, inverse_ref, out_ref, growth_ref, cross_ref):
    half = PANEL // 2
    cross = product(inverse_ref[...], gram_ref[pl.ds(PANEL + half, PANEL), :])
    cross_ref[...] = cross
    inner = product_t(cross, cross)
    out_ref[pl.ds(0, half), :] = gram_ref[pl.ds(half, half), :] - inner[:half]
    out_ref[pl.ds(half, half), pl.ds(0, half)] = jnp.zeros((half, half), jnp.float32)
    out_ref[pl.ds(half, half), pl.ds(half, half)] = gram_ref[pl.ds(PANEL, half), pl.ds(half, half)] - inner[half:, half:]
    eliminate(out_ref, growth_ref)


def on_chip(kernel, flops, *shapes):
    vmem = pl.BlockSpec(memory_space=pltpu.VMEM)
    return lambda *args: pl.pallas_call(
        kernel,
        out_shape=[jax.ShapeDtypeStruct(shape, jnp.float32) for shape in shapes],
        in_specs=[vmem] * len(args),
        out_specs=[vmem] * len(shapes),
        compiler_params=pltpu.CompilerParams(vmem_limit_bytes=32 * 1024 * 1024),
        cost_estimate=pl.CostEstimate(flops=flops, bytes_accessed=524288, transcendentals=PANEL),
    )(*args)


def on_device(state_prev, state_cur, occupancy, panel_order):
    rows, side, width = state_cur.shape
    current = window(state_prev, state_cur, occupancy)
    flat = current.reshape(rows * side, width)
    first, second = panel_order[0], panel_order[1]
    both = fetch_panels(flat, (first, second))
    (gram,) = on_chip(gram_kernel, 4_000_000_000, (PANEL * 5 // 2, PANEL))(both)
    a, b = [both[:, n].reshape(-1, PANEL) for n in range(2)]
    gram = exchange(gram, "core").sum(axis=0)
    a_late, b_late, gram = lax.optimization_barrier((a, b, gram))
    inner = jnp.concatenate([product_t(a_late, flat), product_t(b_late, flat)], axis=0)
    gram = gather(exchange(gram, "z").sum(axis=0), "z")
    inner, gram = lax.optimization_barrier((core_sum(inner), gram))
    gram = lax.all_gather(gram, "core", axis=0, tiled=True)
    inner = exchange(inner, "z").sum(axis=0)
    square, row = (PANEL, PANEL), (1, PANEL)
    inverse_1, growth_1 = on_chip(first_kernel, 1000, square, row)(gram)
    inner, inverse_1 = lax.optimization_barrier((inner, inverse_1))
    inverse_2, growth_2, cross = on_chip(second_kernel, 1000, square, row, square)(gram, inverse_1)
    inner, inverse_2 = lax.optimization_barrier((gather(inner, "z"), inverse_2))
    inner = lax.all_gather(inner, "core", axis=0, tiled=True)
    ax, bx = inner[:PANEL], inner[PANEL:]
    inner_1 = product(inverse_1, ax)
    inner_2 = product(inverse_2, bx - product_t(cross, inner_1))

    col = lax.axis_index(COL)
    is_first, is_second = col == first, col == second
    eye = jnp.eye(PANEL, dtype=jnp.float32) * (-float(side))
    zero = jnp.zeros_like(eye)
    inner_1 = jnp.where(is_first, eye, jnp.where(is_second, zero, inner_1 * RESCALE))
    inner_2 = jnp.where(is_first, zero, jnp.where(is_second, eye, inner_2 * RESCALE))
    weight_b = product_t(inverse_2, inner_2)
    weight_a = product_t(inverse_1, inner_1 - product(cross, weight_b))
    scale = jnp.where(jnp.logical_or(is_first, is_second), 0.0, RESCALE)
    both = jnp.concatenate([a, b], axis=1)
    weight = jnp.concatenate([weight_a, weight_b], axis=0)
    result = flat * scale - product(both, weight)
    return (result.reshape(rows, side, width), jnp.concatenate([growth_1, growth_2], axis=0))


def solution(mesh):
    mesh = jax.sharding.Mesh(mesh.devices.reshape(8, 2, 4, 8), SITE + COL)
    return jax.shard_map(
        on_device,
        mesh=mesh,
        in_specs=(P(SITE, None, COL), P(SITE, None, COL), P(), P()),
        out_specs=(P(SITE, None, COL), P()),
        check_vma=False,
    )
```

```python
import functools

import jax
import jax.numpy as jnp
from jax import lax
from jax.experimental import pallas as pl
from jax.experimental.pallas import tpu as pltpu
from jax.sharding import PartitionSpec as P

STEPS = 4
PANEL = 256
ENERGY = 0.5
RESCALE = 0.015625
BLOCK = 8
GROUP = 4

SITE = ("z", "core")
COL = ("x", "y")


def exchange(value, axis):
    size = lax.axis_size(axis)
    out = lax.all_to_all(value, axis, 0, 0, tiled=True)
    return out.reshape((size, value.shape[0] // size) + value.shape[1:])


def gather(value, axis):
    size = lax.axis_size(axis)
    copies = jnp.broadcast_to(value[None], (size,) + value.shape)
    return lax.all_to_all(copies.reshape((-1,) + value.shape[1:]), axis, 0, 0, tiled=True)


def edge_kernel(far, previous_ref, current_ref, out_ref, sems):
    rows, depth = current_ref.shape[0], STEPS
    core = lax.axis_index("core")
    side = core if far else 1 - core
    old = previous_ref.at[pl.ds(side * (rows - depth + 1), depth - 1)]
    new = current_ref.at[pl.ds(side * (rows - depth), depth)]
    copies = [
        pltpu.make_async_copy(old, out_ref.at[pl.ds(0, depth - 1)], sems.at[0]),
        pltpu.make_async_copy(new, out_ref.at[pl.ds(depth - 1, depth)], sems.at[1]),
    ]
    for copy in copies:
        copy.start()
    for copy in copies:
        copy.wait()


def halos(previous, current):
    size = lax.axis_size(SITE)
    out = []
    for far in (True, False):
        edge = pl.pallas_call(
            functools.partial(edge_kernel, far),
            out_shape=jax.ShapeDtypeStruct((2 * STEPS - 1,) + current.shape[1:], jnp.float32),
            in_specs=[pl.BlockSpec(memory_space=pl.ANY)] * 2,
            out_specs=pl.BlockSpec(memory_space=pltpu.VMEM),
            scratch_shapes=[pltpu.SemaphoreType.DMA((2,))],
        )(previous, current)
        swap = [(i, (i + 1 if i % 2 == far else i - 1) % size) for i in range(size)]
        out.append(lax.ppermute(edge, SITE, swap))
    return out


def window_kernel(previous_ref, current_ref, far_ref, near_ref, occupancy_ref, out_ref, even, odd, masks_ref, sem):
    rows, side = current_ref.shape[0], current_ref.shape[1]
    depth = STEPS
    core, size = lax.axis_index("core"), lax.axis_size("z") * lax.axis_size("core")
    site = lax.axis_index("z") * lax.axis_size("core") + core
    fetch = pltpu.make_async_copy(occupancy_ref, masks_ref, sem)
    fetch.start()

    def place(before_ref, after_ref):
        even[pl.ds(0, depth)] = before_ref[pl.ds(depth - 1, depth)]
        even[pl.ds(depth + rows, depth)] = after_ref[pl.ds(depth - 1, depth)]
        odd[pl.ds(1, depth - 1)] = before_ref[pl.ds(0, depth - 1)]
        odd[pl.ds(depth + rows, depth - 1)] = after_ref[pl.ds(0, depth - 1)]

    pl.when(core == 0)(lambda: place(far_ref, near_ref))
    pl.when(core == 1)(lambda: place(near_ref, far_ref))
    fetch.wait()

    slabs = [lax.rem(site + size - 1, size), site, lax.rem(site + 1, size)]
    unread = jnp.zeros((side - len(slabs) * rows, side), jnp.float32)

    for turn in range(STEPS):
        masks = [masks_ref[turn, pl.ds(pl.multiple_of(slab * rows, rows), rows), :].astype(jnp.float32) for slab in slabs]
        weights = jnp.concatenate(masks + [unread], axis=0).T
        current, previous = (even, odd) if turn % 2 == 0 else (odd, even)

        def load(now, row):
            own = depth <= row < depth + rows
            if own and turn == 0:
                return current_ref[row - depth] if now else previous_ref[row - depth]
            if own and turn == 1 and not now:
                return current_ref[row - depth]
            return (current if now else previous)[row]

        for row in range(turn + 1, rows + 2 * depth - 1 - turn):
            here = load(True, row)
            neighbours = load(True, row + 1) + load(True, row - 1) + pltpu.roll(here, 1, 0) + pltpu.roll(here, side - 1, 0)
            column = row + rows - depth
            value = weights[:, column : column + 1] * (ENERGY * here - neighbours - load(False, row))
            if turn == STEPS - 1:
                out_ref[row - depth] = value
            else:
                previous[row] = value


def window(previous, current, occupancy):
    rows, side, width = current.shape
    slab = pltpu.VMEM((rows + 2 * STEPS, side, width), jnp.float32)
    return pl.pallas_call(
        window_kernel,
        out_shape=jax.ShapeDtypeStruct(current.shape, jnp.float32),
        in_specs=[pl.BlockSpec(memory_space=pltpu.VMEM)] * 4 + [pl.BlockSpec(memory_space=pl.ANY)],
        out_specs=pl.BlockSpec(memory_space=pltpu.VMEM),
        scratch_shapes=[slab, slab, pltpu.VMEM(occupancy.shape, jnp.int32), pltpu.SemaphoreType.DMA],
        compiler_params=pltpu.CompilerParams(vmem_limit_bytes=32 * 1024 * 1024),
        cost_estimate=pl.CostEstimate(flops=12_000_000, bytes_accessed=6_000_000, transcendentals=0),
    )(previous, current, *halos(previous, current), occupancy)


def core_sum(value):
    core, half = lax.axis_index("core"), value.shape[0] // 2
    give = lax.dynamic_slice_in_dim(value, (1 - core) * half, half, 0)
    keep = lax.dynamic_slice_in_dim(value, core * half, half, 0)
    return keep + lax.ppermute(give, "core", [(0, 1), (1, 0)])


def product(left, right):
    return jnp.dot(left, right, precision=lax.Precision.HIGHEST, preferred_element_type=jnp.float32)


def product_t(left, right):
    dims = (((0,), (0,)), ((), ()))
    return lax.dot_general(left, right, dims, precision=lax.Precision.HIGHEST, preferred_element_type=jnp.float32)


def fetch_panels(flat, panels):
    received = exchange(flat, COL)
    mine = jnp.concatenate([lax.dynamic_index_in_dim(received, panel, 0, False) for panel in panels], axis=0)
    both = gather(mine, COL)
    return both.reshape(-1, len(panels), received.shape[1], PANEL)


def split3(x):
    high = x.astype(jnp.bfloat16).astype(jnp.float32)
    rest = x - high
    mid = rest.astype(jnp.bfloat16).astype(jnp.float32)
    return high, mid, rest - mid


def outer(left, right):
    a, b, c = split3(left)
    d, e, f = split3(right)
    lhs = jnp.concatenate([a, a, b, a, c, b], axis=0).astype(jnp.bfloat16)
    rhs = jnp.concatenate([d, e, d, f, d, e], axis=0).astype(jnp.bfloat16)
    return lax.dot_general(lhs, rhs, (((0,), (0,)), ((), ())), preferred_element_type=jnp.float32)


def columns_of(rows, lane, first):
    out = []
    for m in range(BLOCK):
        column = jnp.sum(jnp.where(lane == first + m, rows, 0.0), axis=1, keepdims=True)
        out.append(jnp.broadcast_to(column, (BLOCK, 128)))
    return out


def invert_block(columns):
    entry = {}
    for m in range(BLOCK):
        for i in range(m, BLOCK):
            entry[i, m] = jnp.broadcast_to(columns[m][i : i + 1], (BLOCK, 128))
    inv = {}
    for k in range(BLOCK):
        root = lax.rsqrt(entry[k, k])
        for i in range(k + 1, BLOCK):
            entry[i, k] = entry[i, k] * root
        for m in range(k + 1, BLOCK):
            for i in range(m, BLOCK):
                entry[i, m] = entry[i, m] - entry[i, k] * entry[m, k]
        for c in range(k):
            acc = entry[k, c] * inv[c, c]
            for m in range(c + 1, k):
                acc = acc + entry[k, m] * inv[m, c]
            inv[k, c] = -root * acc
        inv[k, k] = root
    return inv


def combine(columns, rows):
    n = rows.shape[1]
    out = None
    for k in range(BLOCK):
        wide = jnp.concatenate([columns[k]] * (n // 128), axis=1)
        term = wide * jnp.broadcast_to(rows[k : k + 1], (BLOCK, n))
        out = term if out is None else out + term
    return out


def eliminate(out_ref, growth_ref):
    n = out_ref.shape[0]
    lane = lax.broadcasted_iota(jnp.int32, (BLOCK, n), 1)
    sub = lax.broadcasted_iota(jnp.int32, (BLOCK, n), 0)
    sub1 = lax.broadcasted_iota(jnp.int32, (BLOCK, 128), 0)
    lane_all = lax.broadcasted_iota(jnp.int32, (n, n), 1)
    width = GROUP * BLOCK

    def step(j, _):
        first = pl.multiple_of(j * width, width)
        end = first + width
        panels = [out_ref[pl.ds(first + g * BLOCK, BLOCK), :] for g in range(GROUP)]
        done, ahead, rest = [], [], []
        for g in range(GROUP):
            r = first + g * BLOCK
            panel = panels[g]
            inside = jnp.logical_and(lane >= r, lane < r + BLOCK)
            inv = invert_block(columns_of(panel, lane, r))
            below = [columns_of(panels[h], lane, r) for h in range(g + 1, GROUP)]
            panel = jnp.where(inside, jnp.where(lane - r == sub, 1.0, 0.0), panel)
            factor_columns = []
            for k in range(BLOCK):
                column = jnp.zeros((BLOCK, 128), jnp.float32)
                for i in range(k, BLOCK):
                    column = jnp.where(sub1 == i, inv[i, k], column)
                factor_columns.append(column)
            new = combine(factor_columns, panel)
            for h in range(g + 1, GROUP):
                source = below[h - g - 1]
                weights = []
                for k in range(BLOCK):
                    acc = inv[k, 0] * source[0]
                    for m in range(1, k + 1):
                        acc = acc + inv[k, m] * source[m]
                    weights.append(acc)
                panels[h] = jnp.where(inside, 0.0, panels[h]) - combine(weights, new)
            done.append(jnp.where(lane < r + BLOCK, new, 0.0))
            ahead.append(jnp.where(lane >= end, new, 0.0))
            rest.append(jnp.where(jnp.logical_and(lane >= r + BLOCK, lane < end), 0.0, new))
        inside = jnp.logical_and(lane_all >= first, lane_all < end)
        update = outer(jnp.concatenate(ahead, axis=0), jnp.concatenate(rest, axis=0))
        out_ref[...] = jnp.where(inside, 0.0, out_ref[...]) - update
        for g in range(GROUP):
            out_ref[pl.ds(first + g * BLOCK, BLOCK), :] = done[g]
        return 0

    lax.fori_loop(0, n // width, step, 0)
    row = lax.broadcasted_iota(jnp.int32, (n, n), 0)
    growth_ref[...] = -jnp.log(jnp.sum(jnp.where(row == lane_all, out_ref[...], 0.0), axis=0, keepdims=True))


def gram_kernel(both_ref, out_ref):
    half = PANEL // 2
    a, b = [both_ref[:, n].reshape(-1, PANEL) for n in range(2)]
    out_ref[pl.ds(0, half), :] = product_t(a[:, :half], a)
    out_ref[pl.ds(half, half), :] = product_t(b[:, :half], b)
    out_ref[pl.ds(PANEL, half), pl.ds(0, half)] = product_t(a[:, half:], a[:, half:])
    out_ref[pl.ds(PANEL, half), pl.ds(half, half)] = product_t(b[:, half:], b[:, half:])
    out_ref[pl.ds(PANEL + half, PANEL), :] = product_t(a, b)


def first_kernel(gram_ref, out_ref, growth_ref):
    half = PANEL // 2
    out_ref[pl.ds(0, half), :] = gram_ref[pl.ds(0, half), :]
    out_ref[pl.ds(half, half), pl.ds(0, half)] = jnp.zeros((half, half), jnp.float32)
    out_ref[pl.ds(half, half), pl.ds(half, half)] = gram_ref[pl.ds(PANEL, half), pl.ds(0, half)]
    eliminate(out_ref, growth_ref)


def second_kernel(gram_ref, inverse_ref, out_ref, growth_ref, cross_ref):
    half = PANEL // 2
    cross = product(inverse_ref[...], gram_ref[pl.ds(PANEL + half, PANEL), :])
    cross_ref[...] = cross
    inner = product_t(cross, cross)
    out_ref[pl.ds(0, half), :] = gram_ref[pl.ds(half, half), :] - inner[:half]
    out_ref[pl.ds(half, half), pl.ds(0, half)] = jnp.zeros((half, half), jnp.float32)
    out_ref[pl.ds(half, half), pl.ds(half, half)] = gram_ref[pl.ds(PANEL, half), pl.ds(half, half)] - inner[half:, half:]
    eliminate(out_ref, growth_ref)


def on_chip(kernel, flops, *shapes):
    vmem = pl.BlockSpec(memory_space=pltpu.VMEM)
    return lambda *args: pl.pallas_call(
        kernel,
        out_shape=[jax.ShapeDtypeStruct(shape, jnp.float32) for shape in shapes],
        in_specs=[vmem] * len(args),
        out_specs=[vmem] * len(shapes),
        compiler_params=pltpu.CompilerParams(vmem_limit_bytes=32 * 1024 * 1024),
        cost_estimate=pl.CostEstimate(flops=flops, bytes_accessed=524288, transcendentals=PANEL),
    )(*args)


def on_device(state_prev, state_cur, occupancy, panel_order):
    rows, side, width = state_cur.shape
    current = window(state_prev, state_cur, occupancy)
    flat = current.reshape(rows * side, width)
    first, second = panel_order[0], panel_order[1]
    both = fetch_panels(flat, (first, second))
    (gram,) = on_chip(gram_kernel, 4_000_000_000, (PANEL * 5 // 2, PANEL))(both)
    a, b = [both[:, n].reshape(-1, PANEL) for n in range(2)]
    gram = exchange(gram, "core").sum(axis=0)
    a_late, b_late, gram = lax.optimization_barrier((a, b, gram))
    inner = jnp.concatenate([product_t(a_late, flat), product_t(b_late, flat)], axis=0)
    gram = gather(exchange(gram, "z").sum(axis=0), "z")
    inner, gram = lax.optimization_barrier((core_sum(inner), gram))
    gram = lax.all_gather(gram, "core", axis=0, tiled=True)
    inner = exchange(inner, "z").sum(axis=0)
    square, row = (PANEL, PANEL), (1, PANEL)
    inverse_1, growth_1 = on_chip(first_kernel, 1000, square, row)(gram)
    inner, inverse_1 = lax.optimization_barrier((inner, inverse_1))
    inverse_2, growth_2, cross = on_chip(second_kernel, 1000, square, row, square)(gram, inverse_1)
    inner, inverse_2 = lax.optimization_barrier((gather(inner, "z"), inverse_2))
    inner = lax.all_gather(inner, "core", axis=0, tiled=True)
    ax, bx = inner[:PANEL], inner[PANEL:]
    inner_1 = product(inverse_1, ax)
    inner_2 = product(inverse_2, bx - product_t(cross, inner_1))

    col = lax.axis_index(COL)
    is_first, is_second = col == first, col == second
    eye = jnp.eye(PANEL, dtype=jnp.float32) * (-float(side))
    zero = jnp.zeros_like(eye)
    inner_1 = jnp.where(is_first, eye, jnp.where(is_second, zero, inner_1 * RESCALE))
    inner_2 = jnp.where(is_first, zero, jnp.where(is_second, eye, inner_2 * RESCALE))
    weight_b = product_t(inverse_2, inner_2)
    weight_a = product_t(inverse_1, inner_1 - product(cross, weight_b))
    scale = jnp.where(jnp.logical_or(is_first, is_second), 0.0, RESCALE)
    both = jnp.concatenate([a, b], axis=1)
    weight = jnp.concatenate([weight_a, weight_b], axis=0)
    result = flat * scale - product(both, weight)
    return (result.reshape(rows, side, width), jnp.concatenate([growth_1, growth_2], axis=0))


def solution(mesh):
    mesh = jax.sharding.Mesh(mesh.devices.reshape(8, 2, 4, 8), SITE + COL)
    return jax.shard_map(
        on_device,
        mesh=mesh,
        in_specs=(P(SITE, None, COL), P(SITE, None, COL), P(), P()),
        out_specs=(P(SITE, None, COL), P()),
        check_vma=False,
    )
```

```python
import functools

import jax
import jax.numpy as jnp
from jax import lax
from jax.experimental import pallas as pl
from jax.experimental.pallas import tpu as pltpu
from jax.sharding import PartitionSpec as P

STEPS = 4
PANEL = 256
ENERGY = 0.5
RESCALE = 0.015625
BLOCK = 8
GROUP = 4

SITE = ("z", "core")
COL = ("x", "y")


def exchange(value, axis):
    size = lax.axis_size(axis)
    out = lax.all_to_all(value, axis, 0, 0, tiled=True)
    return out.reshape((size, value.shape[0] // size) + value.shape[1:])


def gather(value, axis):
    size = lax.axis_size(axis)
    copies = jnp.broadcast_to(value[None], (size,) + value.shape)
    return lax.all_to_all(copies.reshape((-1,) + value.shape[1:]), axis, 0, 0, tiled=True)


def edge_kernel(far, previous_ref, current_ref, out_ref, sems):
    rows, depth = current_ref.shape[0], STEPS
    core = lax.axis_index("core")
    side = core if far else 1 - core
    old = previous_ref.at[pl.ds(side * (rows - depth + 1), depth - 1)]
    new = current_ref.at[pl.ds(side * (rows - depth), depth)]
    copies = [
        pltpu.make_async_copy(old, out_ref.at[pl.ds(0, depth - 1)], sems.at[0]),
        pltpu.make_async_copy(new, out_ref.at[pl.ds(depth - 1, depth)], sems.at[1]),
    ]
    for copy in copies:
        copy.start()
    for copy in copies:
        copy.wait()


def halos(previous, current):
    size = lax.axis_size(SITE)
    out = []
    for far in (True, False):
        edge = pl.pallas_call(
            functools.partial(edge_kernel, far),
            out_shape=jax.ShapeDtypeStruct((2 * STEPS - 1,) + current.shape[1:], jnp.float32),
            in_specs=[pl.BlockSpec(memory_space=pl.ANY)] * 2,
            out_specs=pl.BlockSpec(memory_space=pltpu.VMEM),
            scratch_shapes=[pltpu.SemaphoreType.DMA((2,))],
        )(previous, current)
        swap = [(i, (i + 1 if i % 2 == far else i - 1) % size) for i in range(size)]
        out.append(lax.ppermute(edge, SITE, swap))
    return out


def window_kernel(previous_ref, current_ref, far_ref, near_ref, occupancy_ref, out_ref, even, odd, masks_ref, sem):
    rows, side = current_ref.shape[0], current_ref.shape[1]
    depth = STEPS
    core, size = lax.axis_index("core"), lax.axis_size("z") * lax.axis_size("core")
    site = lax.axis_index("z") * lax.axis_size("core") + core
    fetch = pltpu.make_async_copy(occupancy_ref, masks_ref, sem)
    fetch.start()

    def place(before_ref, after_ref):
        even[pl.ds(0, depth)] = before_ref[pl.ds(depth - 1, depth)]
        even[pl.ds(depth + rows, depth)] = after_ref[pl.ds(depth - 1, depth)]
        odd[pl.ds(1, depth - 1)] = before_ref[pl.ds(0, depth - 1)]
        odd[pl.ds(depth + rows, depth - 1)] = after_ref[pl.ds(0, depth - 1)]

    pl.when(core == 0)(lambda: place(far_ref, near_ref))
    pl.when(core == 1)(lambda: place(near_ref, far_ref))
    fetch.wait()

    slabs = [lax.rem(site + size - 1, size), site, lax.rem(site + 1, size)]
    unread = jnp.zeros((side - len(slabs) * rows, side), jnp.float32)

    for turn in range(STEPS):
        masks = [masks_ref[turn, pl.ds(pl.multiple_of(slab * rows, rows), rows), :].astype(jnp.float32) for slab in slabs]
        weights = jnp.concatenate(masks + [unread], axis=0).T
        current, previous = (even, odd) if turn % 2 == 0 else (odd, even)

        def load(now, row):
            own = depth <= row < depth + rows
            if own and turn == 0:
                return current_ref[row - depth] if now else previous_ref[row - depth]
            if own and turn == 1 and not now:
                return current_ref[row - depth]
            return (current if now else previous)[row]

        for row in range(turn + 1, rows + 2 * depth - 1 - turn):
            here = load(True, row)
            neighbours = load(True, row + 1) + load(True, row - 1) + pltpu.roll(here, 1, 0) + pltpu.roll(here, side - 1, 0)
            column = row + rows - depth
            value = weights[:, column : column + 1] * (ENERGY * here - neighbours - load(False, row))
            if turn == STEPS - 1:
                out_ref[row - depth] = value
            else:
                previous[row] = value


def window(previous, current, occupancy):
    rows, side, width = current.shape
    slab = pltpu.VMEM((rows + 2 * STEPS, side, width), jnp.float32)
    return pl.pallas_call(
        window_kernel,
        out_shape=jax.ShapeDtypeStruct(current.shape, jnp.float32),
        in_specs=[pl.BlockSpec(memory_space=pltpu.VMEM)] * 4 + [pl.BlockSpec(memory_space=pl.ANY)],
        out_specs=pl.BlockSpec(memory_space=pltpu.VMEM),
        scratch_shapes=[slab, slab, pltpu.VMEM(occupancy.shape, jnp.int32), pltpu.SemaphoreType.DMA],
        compiler_params=pltpu.CompilerParams(vmem_limit_bytes=32 * 1024 * 1024),
        cost_estimate=pl.CostEstimate(flops=12_000_000, bytes_accessed=6_000_000, transcendentals=0),
    )(previous, current, *halos(previous, current), occupancy)


def core_sum(value):
    core, half = lax.axis_index("core"), value.shape[0] // 2
    give = lax.dynamic_slice_in_dim(value, (1 - core) * half, half, 0)
    keep = lax.dynamic_slice_in_dim(value, core * half, half, 0)
    return keep + lax.ppermute(give, "core", [(0, 1), (1, 0)])


def product(left, right):
    return jnp.dot(left, right, precision=lax.Precision.HIGHEST, preferred_element_type=jnp.float32)


def product_t(left, right):
    dims = (((0,), (0,)), ((), ()))
    return lax.dot_general(left, right, dims, precision=lax.Precision.HIGHEST, preferred_element_type=jnp.float32)


def fetch_panels(flat, panels):
    received = exchange(flat, COL)
    mine = jnp.concatenate([lax.dynamic_index_in_dim(received, panel, 0, False) for panel in panels], axis=0)
    both = gather(gather(mine, "y"), "x")
    return both.reshape(-1, len(panels), received.shape[1], PANEL)


def split3(x):
    high = x.astype(jnp.bfloat16).astype(jnp.float32)
    rest = x - high
    mid = rest.astype(jnp.bfloat16).astype(jnp.float32)
    return high, mid, rest - mid


def outer(left, right):
    a, b, c = split3(left)
    d, e, f = split3(right)
    lhs = jnp.concatenate([a, a, b, a, c, b], axis=0).astype(jnp.bfloat16)
    rhs = jnp.concatenate([d, e, d, f, d, e], axis=0).astype(jnp.bfloat16)
    return lax.dot_general(lhs, rhs, (((0,), (0,)), ((), ())), preferred_element_type=jnp.float32)


def columns_of(rows, lane, first):
    out = []
    for m in range(BLOCK):
        column = jnp.sum(jnp.where(lane == first + m, rows, 0.0), axis=1, keepdims=True)
        out.append(jnp.broadcast_to(column, (BLOCK, 128)))
    return out


def invert_block(columns):
    entry = {}
    for m in range(BLOCK):
        for i in range(m, BLOCK):
            entry[i, m] = jnp.broadcast_to(columns[m][i : i + 1], (BLOCK, 128))
    inv = {}
    for k in range(BLOCK):
        root = lax.rsqrt(entry[k, k])
        for i in range(k + 1, BLOCK):
            entry[i, k] = entry[i, k] * root
        for m in range(k + 1, BLOCK):
            for i in range(m, BLOCK):
                entry[i, m] = entry[i, m] - entry[i, k] * entry[m, k]
        for c in range(k):
            acc = entry[k, c] * inv[c, c]
            for m in range(c + 1, k):
                acc = acc + entry[k, m] * inv[m, c]
            inv[k, c] = -root * acc
        inv[k, k] = root
    return inv


def combine(columns, rows):
    n = rows.shape[1]
    out = None
    for k in range(BLOCK):
        wide = jnp.concatenate([columns[k]] * (n // 128), axis=1)
        term = wide * jnp.broadcast_to(rows[k : k + 1], (BLOCK, n))
        out = term if out is None else out + term
    return out


def eliminate(out_ref, growth_ref):
    n = out_ref.shape[0]
    lane = lax.broadcasted_iota(jnp.int32, (BLOCK, n), 1)
    sub = lax.broadcasted_iota(jnp.int32, (BLOCK, n), 0)
    sub1 = lax.broadcasted_iota(jnp.int32, (BLOCK, 128), 0)
    lane_all = lax.broadcasted_iota(jnp.int32, (n, n), 1)
    width = GROUP * BLOCK

    def step(j, _):
        first = pl.multiple_of(j * width, width)
        end = first + width
        panels = [out_ref[pl.ds(first + g * BLOCK, BLOCK), :] for g in range(GROUP)]
        done, ahead, rest = [], [], []
        for g in range(GROUP):
            r = first + g * BLOCK
            panel = panels[g]
            inside = jnp.logical_and(lane >= r, lane < r + BLOCK)
            inv = invert_block(columns_of(panel, lane, r))
            below = [columns_of(panels[h], lane, r) for h in range(g + 1, GROUP)]
            panel = jnp.where(inside, jnp.where(lane - r == sub, 1.0, 0.0), panel)
            factor_columns = []
            for k in range(BLOCK):
                column = jnp.zeros((BLOCK, 128), jnp.float32)
                for i in range(k, BLOCK):
                    column = jnp.where(sub1 == i, inv[i, k], column)
                factor_columns.append(column)
            new = combine(factor_columns, panel)
            for h in range(g + 1, GROUP):
                source = below[h - g - 1]
                weights = []
                for k in range(BLOCK):
                    acc = inv[k, 0] * source[0]
                    for m in range(1, k + 1):
                        acc = acc + inv[k, m] * source[m]
                    weights.append(acc)
                panels[h] = jnp.where(inside, 0.0, panels[h]) - combine(weights, new)
            done.append(jnp.where(lane < r + BLOCK, new, 0.0))
            ahead.append(jnp.where(lane >= end, new, 0.0))
            rest.append(jnp.where(jnp.logical_and(lane >= r + BLOCK, lane < end), 0.0, new))
        inside = jnp.logical_and(lane_all >= first, lane_all < end)
        update = outer(jnp.concatenate(ahead, axis=0), jnp.concatenate(rest, axis=0))
        out_ref[...] = jnp.where(inside, 0.0, out_ref[...]) - update
        for g in range(GROUP):
            out_ref[pl.ds(first + g * BLOCK, BLOCK), :] = done[g]
        return 0

    lax.fori_loop(0, n // width, step, 0)
    row = lax.broadcasted_iota(jnp.int32, (n, n), 0)
    growth_ref[...] = -jnp.log(jnp.sum(jnp.where(row == lane_all, out_ref[...], 0.0), axis=0, keepdims=True))


def gram_kernel(both_ref, out_ref):
    half = PANEL // 2
    a, b = [both_ref[:, n].reshape(-1, PANEL) for n in range(2)]
    out_ref[pl.ds(0, half), :] = product_t(a[:, :half], a)
    out_ref[pl.ds(half, half), :] = product_t(b[:, :half], b)
    out_ref[pl.ds(PANEL, half), pl.ds(0, half)] = product_t(a[:, half:], a[:, half:])
    out_ref[pl.ds(PANEL, half), pl.ds(half, half)] = product_t(b[:, half:], b[:, half:])
    out_ref[pl.ds(PANEL + half, PANEL), :] = product_t(a, b)


def sum_copies_kernel(parts_ref, out_ref):
    total = parts_ref[0]
    for n in range(1, parts_ref.shape[0]):
        total = total + parts_ref[n]
    for n in range(out_ref.shape[0]):
        out_ref[n] = total


def first_kernel(gram_ref, out_ref, growth_ref):
    half = PANEL // 2
    out_ref[pl.ds(0, half), :] = gram_ref[pl.ds(0, half), :]
    out_ref[pl.ds(half, half), pl.ds(0, half)] = jnp.zeros((half, half), jnp.float32)
    out_ref[pl.ds(half, half), pl.ds(half, half)] = gram_ref[pl.ds(PANEL, half), pl.ds(0, half)]
    eliminate(out_ref, growth_ref)


def second_kernel(gram_ref, inverse_ref, out_ref, growth_ref, cross_ref):
    half = PANEL // 2
    cross = product(inverse_ref[...], gram_ref[pl.ds(PANEL + half, PANEL), :])
    cross_ref[...] = cross
    inner = product_t(cross, cross)
    out_ref[pl.ds(0, half), :] = gram_ref[pl.ds(half, half), :] - inner[:half]
    out_ref[pl.ds(half, half), pl.ds(0, half)] = jnp.zeros((half, half), jnp.float32)
    out_ref[pl.ds(half, half), pl.ds(half, half)] = gram_ref[pl.ds(PANEL, half), pl.ds(half, half)] - inner[half:, half:]
    eliminate(out_ref, growth_ref)


def on_chip(kernel, flops, *shapes):
    vmem = pl.BlockSpec(memory_space=pltpu.VMEM)
    return lambda *args: pl.pallas_call(
        kernel,
        out_shape=[jax.ShapeDtypeStruct(shape, jnp.float32) for shape in shapes],
        in_specs=[vmem] * len(args),
        out_specs=[vmem] * len(shapes),
        compiler_params=pltpu.CompilerParams(vmem_limit_bytes=32 * 1024 * 1024),
        cost_estimate=pl.CostEstimate(flops=flops, bytes_accessed=524288, transcendentals=PANEL),
    )(*args)


def sum_and_gather(parts, axis):
    (copies,) = on_chip(sum_copies_kernel, 1000, parts.shape)(parts)
    return lax.all_to_all(copies.reshape(-1, PANEL), axis, 0, 0, tiled=True)


def on_device(state_prev, state_cur, occupancy, panel_order):
    rows, side, width = state_cur.shape
    current = window(state_prev, state_cur, occupancy)
    flat = current.reshape(rows * side, width)
    first, second = panel_order[0], panel_order[1]
    both = fetch_panels(flat, (first, second))
    (gram,) = on_chip(gram_kernel, 4_000_000_000, (PANEL * 5 // 2, PANEL))(both)
    a, b = [both[:, n].reshape(-1, PANEL) for n in range(2)]
    gram = exchange(gram, "core").sum(axis=0)
    a_late, b_late, gram = lax.optimization_barrier((a, b, gram))
    inner = jnp.concatenate([product_t(a_late, flat), product_t(b_late, flat)], axis=0)
    gram = sum_and_gather(exchange(gram, "z"), "z")
    inner, gram = lax.optimization_barrier((core_sum(inner), gram))
    gram = lax.all_gather(gram, "core", axis=0, tiled=True)
    inner = exchange(inner, "z")
    square, row = (PANEL, PANEL), (1, PANEL)
    inverse_1, growth_1 = on_chip(first_kernel, 1000, square, row)(gram)
    inner, inverse_1 = lax.optimization_barrier((inner, inverse_1))
    inverse_2, growth_2, cross = on_chip(second_kernel, 1000, square, row, square)(gram, inverse_1)
    inner, inverse_2 = lax.optimization_barrier((sum_and_gather(inner, "z"), inverse_2))
    inner = lax.all_gather(inner, "core", axis=0, tiled=True)
    ax, bx = inner[:PANEL], inner[PANEL:]
    inner_1 = product(inverse_1, ax)
    inner_2 = product(inverse_2, bx - product_t(cross, inner_1))

    col = lax.axis_index(COL)
    is_first, is_second = col == first, col == second
    eye = jnp.eye(PANEL, dtype=jnp.float32) * (-float(side))
    zero = jnp.zeros_like(eye)
    inner_1 = jnp.where(is_first, eye, jnp.where(is_second, zero, inner_1 * RESCALE))
    inner_2 = jnp.where(is_first, zero, jnp.where(is_second, eye, inner_2 * RESCALE))
    weight_b = product_t(inverse_2, inner_2)
    weight_a = product_t(inverse_1, inner_1 - product(cross, weight_b))
    scale = jnp.where(jnp.logical_or(is_first, is_second), 0.0, RESCALE)
    both = jnp.concatenate([a, b], axis=1)
    weight = jnp.concatenate([weight_a, weight_b], axis=0)
    result = flat * scale - product(both, weight)
    return (result.reshape(rows, side, width), jnp.concatenate([growth_1, growth_2], axis=0))


def solution(mesh):
    mesh = jax.sharding.Mesh(mesh.devices.reshape(8, 2, 4, 8), SITE + COL)
    return jax.shard_map(
        on_device,
        mesh=mesh,
        in_specs=(P(SITE, None, COL), P(SITE, None, COL), P(), P()),
        out_specs=(P(SITE, None, COL), P()),
        check_vma=False,
    )
```
